32 devices in a mesh: dp: 8 (over z, y), tensor: 4 (over x, core).
Axes of the slice: x: 2, y: 2, z: 4, core: 2. Of those that a mesh axis runs over, the one named last changes fastest.
Arguments:
- master: float32 [2, 8192, 2048], P(None, 'dp', 'tensor'), may hold values from -0.0625 to 0.0625
- momentum: float32 [2, 8192, 2048], P(None, 'dp', 'tensor'), may hold values from -6 to 6
- gradient: float32 [2, 8192, 2048], P(None, 'dp', 'tensor'), may hold values from -60 to 60
- bucket_table: int32 [4, 8], P('tensor'), may hold values from 0 to 3, as said below
- tokens: bfloat16 [2048, 8192], P('dp', 'tensor'), may hold values from -6 to 6
- norm_gain: float32 [8192], replicated, may hold values from 0.1 to 1.9
Outputs:
- new_master: float32 [2, 8192, 2048], P(None, 'dp', 'tensor')
- new_momentum: float32 [2, 8192, 2048], P(None, 'dp', 'tensor')
- key_values: bfloat16 [2048, 2048], P('dp', 'tensor')
The draws below stay inside these ranges and needn't reach their ends.
Inputs may be any that keep to these rules, and one draw needn't show every extreme that they name: `bucket_table`: in each row of 8 entries every value from 0 to 3 appears exactly twice.
All inputs are finite; a program needn't handle non-finite values.
Results may differ from the reference program's by a relative error of at most 0.001.
The reference program's roundings to bfloat16 on the way (of `normed` and `first_weights`) count: a program that leaves them out, or rounds other values in their place, can miss the bound.
Values may be sent and summed in bfloat16 or wider, within the bound.
No kernel may reach another device: no remote copies, remote signals or barrier semaphores. Data moves between devices by JAX's collectives and lax.ppermute only.
A program may use at most 128 MiB of HBM per device.

```python
import math
import jax
import jax.numpy as jnp
from jax import lax

D = 8192
HD = 128
LAYERS = 2
NS_ITERS = 3
TOKENS = 2048
GROUPS = 4
MATS = 8
KVCOLS = 2048


def draw_gradient(key, part):
    key_list = jax.random.split(jax.random.fold_in(key, 11), 3)
    spread = math.log(10.0)
    row_scale = jnp.exp(jax.random.uniform(key_list[0], (LAYERS, D, 1), minval=-0.5 * spread, maxval=0.5 * spread))
    ramp_scale = (0.5 + jnp.arange(D, dtype=jnp.float32) / (D - 1)).reshape(1, D, 1)
    col_scale = jnp.exp(jax.random.uniform(key_list[1], (LAYERS, 1, KVCOLS), minval=-0.5 * spread, maxval=0.5 * spread))
    values = jax.random.truncated_normal(key_list[2], -4.0, 4.0, (LAYERS, D, KVCOLS), jnp.float32)
    return (values * row_scale * ramp_scale * col_scale).astype(jnp.float32)


def draw_bucket_table(key, part):
    group_keys = jax.random.split(jax.random.fold_in(key, 23), GROUPS)

    def one_group(group_key):
        order_ids = jax.random.permutation(group_key, MATS)
        position = jnp.argsort(order_ids)
        return (position // 2).astype(jnp.int32)
    return jax.vmap(one_group)(group_keys)


def steps_of(own_key, extent, shards, low, high):
    def one(dim, parts):
        draws = jax.random.uniform(jax.random.fold_in(jax.random.fold_in(own_key, 6), dim), (parts,), jnp.float32, low / len(shards), high / len(shards))
        return jnp.repeat(jnp.exp(draws), extent[dim] // parts).reshape((-1,) + (1,) * (len(extent) - dim - 1))

    level = one(*shards[0])
    for cut in shards[1:]:
        level = level * one(*cut)
    return level


def noise(key, dims, scale, bound, shards=(), held_as=jnp.bfloat16):
    array = jax.random.normal(key, dims, jnp.float32) * scale
    if len(shards) > 0:
        array = steps_of(key, dims, shards, -0.22, 0.18) * array
    return jnp.clip(array, min=-bound, max=bound).astype(held_as)


def setup_inputs(seed: int = 0) -> dict:
    seeds = jax.random.split(jax.random.key(seed), 7)
    master = noise(seeds[0], (LAYERS, D, KVCOLS), D ** -0.5, 0.0625, ((1, 8), (2, 4)), jnp.float32)
    momentum = noise(seeds[1], (LAYERS, D, KVCOLS), 1.0, 6.0, ((1, 8), (2, 4)), jnp.float32)
    gradient = draw_gradient(jax.random.fold_in(seeds[6], 71), 0)
    bucket_table = draw_bucket_table(jax.random.fold_in(seeds[6], 71), 0)
    tokens = noise(seeds[4], (TOKENS, D), 1.0, 6.0, ((0, 8), (1, 4)))
    norm_gain = jnp.clip(1.0 + 0.18 * jax.random.normal(seeds[5], (D,), jnp.float32), 0.1, 1.9)
    return {"master": master, "momentum": momentum, "gradient": gradient, "bucket_table": bucket_table, "tokens": tokens, "norm_gain": norm_gain}


beta_momentum = 0.95
learn_rate = 0.05
first_coeff = 3.4445
cube_coeff = -4.775
fifth_coeff = 2.0315
frob_epsilon = 1e-07
rms_epsilon = 1e-05

def reference(master, momentum, gradient, bucket_table, tokens, norm_gain):
    new_momentum = beta_momentum * momentum + gradient
    update = gradient + beta_momentum * new_momentum
    groups = bucket_table.shape[0]
    count = bucket_table.shape[1]
    slots = count // LAYERS
    heads = update.reshape(LAYERS, D, groups, slots, HD).transpose(2, 0, 3, 1, 4).reshape(groups, count, D, HD)
    sort_keys = bucket_table * count + jnp.arange(count, dtype=jnp.int32)[None, :]
    order_ids = jnp.argsort(sort_keys, axis=1).astype(jnp.int32)
    picked = jnp.take_along_axis(heads, order_ids[:, :, None, None], axis=1)
    stacked = picked.reshape(groups, count // 2, 2, D, HD).transpose(0, 1, 3, 2, 4).reshape(groups, count // 2, D, 2 * HD)
    norms = jnp.sqrt(lax.optimization_barrier(jnp.sum(stacked * stacked, axis=(2, 3))))
    current = stacked / (norms + frob_epsilon)[:, :, None, None]
    for iteration in range(NS_ITERS):
        gram_mat = jnp.einsum('gbdk,gbdj->gbkj', current, current, precision=lax.Precision.HIGHEST)
        square = jnp.einsum('gbkj,gbjl->gbkl', gram_mat, gram_mat, precision=lax.Precision.HIGHEST)
        factor = cube_coeff * gram_mat + fifth_coeff * square
        current = first_coeff * current + jnp.einsum('gbdk,gbkj->gbdj', current, factor, precision=lax.Precision.HIGHEST)
    split = current.reshape(groups, count // 2, D, 2, HD).transpose(0, 1, 3, 2, 4).reshape(groups, count, D, HD)
    inverse = jnp.argsort(order_ids, axis=1).astype(jnp.int32)
    restored = jnp.take_along_axis(split, inverse[:, :, None, None], axis=1)
    ortho = restored.reshape(groups, LAYERS, slots, D, HD).transpose(1, 3, 0, 2, 4).reshape(LAYERS, D, groups * slots * HD)
    step_scale = learn_rate * math.sqrt(max(1.0, D / (2.0 * HD)))
    new_master = master - step_scale * ortho
    tokens_f = tokens.astype(jnp.float32)
    inv_rms = lax.rsqrt(lax.optimization_barrier(jnp.mean(tokens_f * tokens_f, axis=1, keepdims=True)) + rms_epsilon)
    normed = (tokens_f * inv_rms * norm_gain[None, :]).astype(jnp.bfloat16)
    first_weights = new_master[0].astype(jnp.bfloat16)
    key_values = jnp.dot(normed, first_weights, preferred_element_type=jnp.float32).astype(jnp.bfloat16)
    return (new_master, new_momentum, key_values)
```

```python
import functools
import math

import jax
import jax.numpy as jnp
from jax import lax
from jax.experimental import pallas as pl
from jax.experimental.pallas import tpu as pltpu
from jax.sharding import PartitionSpec as P

HD = 128
NS_ITERS = 3

beta_momentum = 0.95
learn_rate = 0.05
first_coeff = 3.4445
cube_coeff = -4.775
fifth_coeff = 2.0315
frob_epsilon = 1e-07
rms_epsilon = 1e-05

CHUNKS = 2

bf16 = jnp.bfloat16
f32 = jnp.float32
HIGHEST = lax.Precision.HIGHEST


def head_of(table, place, count):
    bucket = place // 2
    lower = jnp.int32(0)
    upper = jnp.int32(0)
    for i in range(count):
        j = count - 1 - i
        lower = jnp.where(table[j] == bucket, j, lower)
        upper = jnp.where(table[i] == bucket, i, upper)
    return jnp.where(place % 2 == 0, lower, upper)


def grid_masks(size):
    rows = lax.broadcasted_iota(jnp.int32, (size, size), 0)
    cols = lax.broadcasted_iota(jnp.int32, (size, size), 1)
    return rows, cols


def pack_symmetric(full):
    half = full.shape[0] // 2
    rows, cols = grid_masks(half)
    low = full[half:, half:]
    mixed = jnp.where(rows <= cols, full[:half, :half], low)
    diag = jnp.sum(jnp.where(rows == cols, low, 0.0), axis=0, keepdims=True)
    return mixed, full[:half, half:], jnp.broadcast_to(diag, (8, half))


def unpack_symmetric(packed):
    half = packed.shape[1]
    mixed = packed[:half]
    side = packed[half : 2 * half]
    diag = packed[2 * half : 2 * half + 1]
    rows, cols = grid_masks(half)
    turned = mixed.T
    first = jnp.where(rows <= cols, mixed, turned)
    low = jnp.where(rows > cols, mixed, jnp.where(rows == cols, diag, turned))
    return jnp.concatenate(
        [
            jnp.concatenate([first, side], axis=1),
            jnp.concatenate([side.T, low], axis=1),
        ],
        axis=0,
    )


def store_packed(ref, full):
    half = full.shape[0] // 2
    mixed, side, diag = pack_symmetric(full)
    ref[0:half, :] = mixed
    ref[half : 2 * half, :] = side
    ref[2 * half : 2 * half + 8, :] = diag


def dot_t(a, b):
    return lax.dot_general(a, b, (((0,), (0,)), ((), ())), preferred_element_type=f32)


def dot_full(a, b):
    return lax.dot_general(
        a, b, (((1,), (0,)), ((), ())), precision=HIGHEST, preferred_element_type=f32
    )


def gram_kernel(table, place, momentum, gradient, new_momentum, update, *rest, parts):
    outs = rest[:parts]
    split = rest[parts]
    step = pl.program_id(0)
    fresh = beta_momentum * momentum[0] + gradient[0]
    new_momentum[0] = fresh
    change = gradient[0] + beta_momentum * fresh
    update[0] = change
    first = change.astype(bf16)
    left = change - first.astype(f32)
    second = left.astype(bf16)
    third = (left - second.astype(f32)).astype(bf16)

    def keep(side):
        cols = slice(side * HD, (side + 1) * HD)
        split[0, :, cols] = first
        split[1, :, cols] = second
        split[2, :, cols] = third

    @pl.when(step % 2 == 0)
    def _():
        keep(0)

    @pl.when(step % 2 == 1)
    def _():
        keep(1)
        one = split[0]
        two = split[1]
        rough = dot_t(one, one) + dot_t(two, two)
        rough = rough + 2.0 * (dot_t(one, two) + dot_t(one, split[2]))
        full = 0.5 * (rough + rough.T)
        mixed, side, diag = pack_symmetric(full)
        away = (step // 2) ^ place[0]
        for k in range(parts):

            @pl.when(away == k)
            def _():
                outs[k][0:HD, :] = mixed
                outs[k][HD : 2 * HD, :] = side
                outs[k][2 * HD : 2 * HD + 8, :] = diag


def local_grams(table, place, momentum, gradient, parts):
    layers, height, width = momentum.shape
    slots = width // HD
    count = layers * slots

    def head_block(p, table, place):
        head = head_of(table, p, count)
        return (head // slots, 0, head % slots)

    block = pl.BlockSpec((1, height, HD), head_block)
    packed = (2 * HD + 8, HD)
    return pl.pallas_call(
        functools.partial(gram_kernel, parts=parts),
        grid_spec=pltpu.PrefetchScalarGridSpec(
            num_scalar_prefetch=2,
            grid=(count,),
            in_specs=[block, block],
            out_specs=[block, pl.BlockSpec((1, height, HD), lambda p, t, q: (p // 2, 0, p % 2))]
            + [pl.BlockSpec(packed, lambda p, t, q: (0, 0))] * parts,
            scratch_shapes=[pltpu.VMEM((3, height, 2 * HD), bf16)],
        ),
        out_shape=[
            jax.ShapeDtypeStruct(momentum.shape, f32),
            jax.ShapeDtypeStruct((count // 2, height, 2 * HD), f32),
        ]
        + [jax.ShapeDtypeStruct(packed, f32)] * parts,
        name="grams",
    )(table, place, momentum, gradient)


def series_kernel(*refs, step_scale):
    out = refs[-1]
    packed = refs[0][...]
    for ref in refs[1:-1]:
        packed = packed + ref[...]
    total = unpack_symmetric(packed)
    rows, cols = grid_masks(total.shape[0])
    on_diag = rows == cols
    trace = jnp.sum(jnp.where(on_diag, total, 0.0), keepdims=True)
    scale = 1.0 / (jnp.sqrt(trace) + frob_epsilon)
    gram = total * (scale * scale)
    product = None
    for iteration in range(NS_ITERS):
        square = dot_full(gram, gram)
        factor = cube_coeff * gram + fifth_coeff * square
        factor = factor + jnp.where(on_diag, first_coeff, 0.0)
        product = factor if product is None else dot_full(product, factor)
        if iteration + 1 < NS_ITERS:
            gram = dot_full(dot_full(gram, factor), factor)
    store_packed(out, product * (scale * step_scale))


def series(pieces, step_scale):
    return pl.pallas_call(
        functools.partial(series_kernel, step_scale=step_scale),
        out_shape=jax.ShapeDtypeStruct(pieces[0].shape, f32),
        name="series",
    )(*pieces)


def apply_kernel(table, place, *refs, parts, slots, count, chunks):
    packed = refs[:parts]
    update, master = refs[parts : parts + 2]
    new_master = refs[parts + 2]
    weights = refs[parts + 3 : parts + 3 + chunks]
    factors, spare = refs[parts + 3 + chunks :]
    step = pl.program_id(0)

    @pl.when(step == 0)
    def _():
        for k in range(parts):
            factors[k ^ place[0]] = unpack_symmetric(packed[k][...])

    head = head_of(table, step, count)

    def finish(ortho):
        fresh = master[0] - ortho
        new_master[0] = fresh
        rounded = fresh.astype(bf16)
        per_chunk = slots // chunks
        for slot in range(slots):

            @pl.when(head == slot)
            def _():
                cols = slice((slot % per_chunk) * HD, (slot % per_chunk + 1) * HD)
                weights[slot // per_chunk][:, cols] = rounded

    @pl.when(step % 2 == 0)
    def _():
        both = dot_full(update[0], factors[step // 2])
        spare[...] = both[:, HD:]
        finish(both[:, :HD])

    @pl.when(step % 2 == 1)
    def _():
        finish(spare[...])


def apply_update(table, place, packed, update, master, chunks):
    layers, height, width = master.shape
    slots = width // HD
    count = layers * slots
    parts = len(packed)

    def head_block(p, table, place):
        head = head_of(table, p, count)
        return (head // slots, 0, head % slots)

    whole = pl.BlockSpec(packed[0].shape, lambda p, t, q: (0, 0))
    block = pl.BlockSpec((1, height, HD), head_block)
    piece = (height, width // chunks)
    return pl.pallas_call(
        functools.partial(apply_kernel, parts=parts, slots=slots, count=count, chunks=chunks),
        grid_spec=pltpu.PrefetchScalarGridSpec(
            num_scalar_prefetch=2,
            grid=(count,),
            in_specs=[whole] * parts
            + [pl.BlockSpec((1, height, 2 * HD), lambda p, t, q: (p // 2, 0, 0)), block],
            out_specs=[block] + [pl.BlockSpec(piece, lambda p, t, q: (0, 0))] * chunks,
            scratch_shapes=[
                pltpu.VMEM((count // 2, 2 * HD, 2 * HD), f32),
                pltpu.VMEM((height, HD), f32),
            ],
        ),
        out_shape=[jax.ShapeDtypeStruct(master.shape, f32)]
        + [jax.ShapeDtypeStruct(piece, bf16)] * chunks,
        name="apply",
    )(table, place, *packed, update, master)


def norm_kernel(place, *refs, parts):
    halves = refs[: 2 * parts]
    inverse, gain, out = refs[2 * parts :]
    height = halves[0].shape[0]
    for k in range(parts):
        away = k ^ place[0] ^ place[1]
        for side in range(2):
            rows = slice(side * height, (side + 1) * height)
            values = halves[2 * k + side][...].astype(f32)
            out[away, rows, :] = (values * inverse[away, rows, :] * gain[...]).astype(bf16)


def normalise(place, halves, inverse, gain):
    parts = len(halves) // 2
    height, width = halves[0].shape
    vmem = pl.BlockSpec(memory_space=pltpu.VMEM)
    return pl.pallas_call(
        functools.partial(norm_kernel, parts=parts),
        in_specs=[pl.BlockSpec(memory_space=pltpu.SMEM)] + [vmem] * (2 * parts + 2),
        out_specs=vmem,
        out_shape=jax.ShapeDtypeStruct((parts, 2 * height, width), bf16),
        name="normalise",
    )(place, *halves, inverse, gain)


def project_kernel(place, normed, *refs, members, parts):
    weights = refs[:members]
    outs = refs[members:]
    step = pl.program_id(0)
    height = weights[0].shape[0]
    total = None
    for k in range(members):
        start = pl.multiple_of((k ^ place[2]) * height, HD)
        part = jnp.dot(
            normed[0, :, pl.ds(start, height)], weights[k][...], preferred_element_type=f32
        )
        total = part if total is None else total + part
    for m in range(parts):

        @pl.when(step == m)
        def _():
            outs[m][...] = total


def project(place, normed, weights):
    parts, height, width = normed.shape
    cols = weights[0].shape[1]
    return pl.pallas_call(
        functools.partial(project_kernel, members=len(weights), parts=parts),
        grid_spec=pltpu.PrefetchScalarGridSpec(
            num_scalar_prefetch=1,
            grid=(parts,),
            in_specs=[pl.BlockSpec((1, height, width), lambda m, q: (m, 0, 0))]
            + [pl.BlockSpec(w.shape, lambda m, q: (0, 0)) for w in weights],
            out_specs=[pl.BlockSpec((height, cols), lambda m, q: (0, 0))] * parts,
        ),
        out_shape=[jax.ShapeDtypeStruct((height, cols), f32)] * parts,
        name="project",
    )(place, normed, *weights)


def per_device(master, momentum, gradient, bucket_table, tokens, norm_gain, *, dp, tp):
    layers, height, width = master.shape
    share = tokens.shape[1]
    features = norm_gain.shape[0]
    count = bucket_table.shape[1]
    parts = tp
    members = dp // parts
    assert count // 2 == parts and share * tp == features and height * dp == features
    mine = lax.axis_index("dp")
    column = lax.axis_index("tensor")
    row = mine // members
    place = jnp.stack([row, column, mine % members]).astype(jnp.int32)
    table = bucket_table[0]

    def swap_dp(value, bits):
        return lax.ppermute(value, "dp", [(i, i ^ bits) for i in range(dp)])

    def swap_tensor(value, bits):
        return lax.ppermute(value, "tensor", [(i, i ^ bits) for i in range(tp)])

    half = tokens.shape[0] // 2
    sent = []
    for side in range(2):
        pairs = []
        for q in range(parts):
            for r in range(members):
                for j in range(tp):
                    target = q ^ (side * (tp // 2))
                    pairs.append(((q * members + r) * tp + j, (j * members + r) * tp + target))
        piece = lax.slice_in_dim(tokens, side * half, (side + 1) * half, axis=0)
        sent.append(lax.ppermute(piece, ("dp", "tensor"), pairs))

    new_momentum, update, *grams = local_grams(table, place, momentum, gradient, parts)

    held = {(0, 0): sent[0], (1, tp // 2): sent[1]}
    bits = tp // 2
    while bits:
        fresh = {}
        for (side, offset), value in held.items():
            fresh[(side, offset ^ bits)] = swap_tensor(value, bits)
        held.update(fresh)
        bits //= 2
    halves = [held[(side, offset)] for offset in range(parts) for side in range(2)]

    local_f = tokens.astype(f32)
    sums = jnp.sum(local_f * local_f, axis=1)
    bits = tp // 2
    while bits:
        sums = sums + swap_tensor(sums, bits)
        bits //= 2
    by_row = [sums] + [swap_dp(sums, k * members) for k in range(1, parts)]
    inverse = lax.rsqrt(jnp.stack(by_row) / features + rms_epsilon)[:, :, None]
    gain = lax.dynamic_slice_in_dim(norm_gain, row * share, share, 0)[None, :]
    normed = normalise(place, halves, inverse, gain)

    total = grams[0]
    for k in range(1, parts):
        total = total + swap_dp(grams[k], k * members)
    pieces = [total]
    bits = 1
    while bits < members:
        pieces = [sum(pieces), swap_dp(sum(pieces), bits)]
        bits *= 2
    step_scale = learn_rate * math.sqrt(max(1.0, features / (2.0 * HD)))
    own = series(pieces, step_scale)
    packed = [own] + [swap_dp(own, k * members) for k in range(1, parts)]
    new_master, *weights = apply_update(table, place, packed, update, master, CHUNKS)

    results = []
    for piece in weights:
        gathered = [piece] + [swap_dp(piece, k) for k in range(1, members)]
        partial = project(place, normed, gathered)
        result = partial[0]
        for k in range(1, parts):
            result = result + swap_dp(partial[k], k * members)
        results.append(result.astype(bf16))
    return (new_master, new_momentum, jnp.concatenate(results, axis=1))


def solution(mesh):
    placed = (
        P(None, "dp", "tensor"),
        P(None, "dp", "tensor"),
        P(None, "dp", "tensor"),
        P("tensor", None),
        P("dp", "tensor"),
        P(),
    )
    return jax.shard_map(
        functools.partial(per_device, dp=mesh.shape["dp"], tp=mesh.shape["tensor"]),
        mesh=mesh,
        in_specs=placed,
        out_specs=(P(None, "dp", "tensor"), P(None, "dp", "tensor"), P("dp", "tensor")),
        check_vma=False,
    )
```

```python
import functools
import math

import jax
import jax.numpy as jnp
from jax import lax
from jax.experimental import pallas as pl
from jax.experimental.pallas import tpu as pltpu
from jax.sharding import PartitionSpec as P

HD = 128
NS_ITERS = 3

beta_momentum = 0.95
learn_rate = 0.05
first_coeff = 3.4445
cube_coeff = -4.775
fifth_coeff = 2.0315
frob_epsilon = 1e-07
rms_epsilon = 1e-05

CHUNKS = 2
ROWS = 256
MIB = 1 << 20

bf16 = jnp.bfloat16
f32 = jnp.float32
HIGHEST = lax.Precision.HIGHEST


def head_of(table, place, count):
    bucket = place // 2
    lower = jnp.int32(0)
    upper = jnp.int32(0)
    for i in range(count):
        j = count - 1 - i
        lower = jnp.where(table[j] == bucket, j, lower)
        upper = jnp.where(table[i] == bucket, i, upper)
    return jnp.where(place % 2 == 0, lower, upper)


def grid_masks(size):
    rows = lax.broadcasted_iota(jnp.int32, (size, size), 0)
    cols = lax.broadcasted_iota(jnp.int32, (size, size), 1)
    return rows, cols


def pack_symmetric(full):
    half = full.shape[0] // 2
    rows, cols = grid_masks(half)
    low = full[half:, half:]
    mixed = jnp.where(rows <= cols, full[:half, :half], low)
    diag = jnp.sum(jnp.where(rows == cols, low, 0.0), axis=0, keepdims=True)
    return mixed, full[:half, half:], jnp.broadcast_to(diag, (8, half))


def unpack_symmetric(packed):
    half = packed.shape[1]
    mixed = packed[:half]
    side = packed[half : 2 * half]
    diag = packed[2 * half : 2 * half + 1]
    rows, cols = grid_masks(half)
    turned = mixed.T
    first = jnp.where(rows <= cols, mixed, turned)
    low = jnp.where(rows > cols, mixed, jnp.where(rows == cols, diag, turned))
    return jnp.concatenate(
        [
            jnp.concatenate([first, side], axis=1),
            jnp.concatenate([side.T, low], axis=1),
        ],
        axis=0,
    )


def store_packed(ref, full):
    half = full.shape[0] // 2
    mixed, side, diag = pack_symmetric(full)
    ref[0:half, :] = mixed
    ref[half : 2 * half, :] = side
    ref[2 * half : 2 * half + 8, :] = diag


def dot_t(a, b):
    return lax.dot_general(a, b, (((0,), (0,)), ((), ())), preferred_element_type=f32)


def dot_full(a, b):
    return lax.dot_general(
        a, b, (((1,), (0,)), ((), ())), precision=HIGHEST, preferred_element_type=f32
    )


def bucket_side(table, head):
    side = jnp.int32(0)
    for i in range(head):
        side = jnp.where(table[i] == table[head], 1, side)
    return side


def gram_kernel(table, place, momentum, gradient, new_momentum, update, *rest, parts, slots):
    outs = rest[:parts]
    split, total = rest[parts:]
    step = pl.program_id(0)
    layers, height, _ = momentum.shape
    wide = 2 * HD
    rows = pl.ds(pl.multiple_of(step * height, height), height)
    for head in range(layers * slots):
        layer = head // slots
        cols = slice((head % slots) * HD, (head % slots + 1) * HD)
        slope = gradient[layer, :, cols]
        fresh = beta_momentum * momentum[layer, :, cols] + slope
        new_momentum[layer, :, cols] = fresh
        change = slope + beta_momentum * fresh
        update[layer, rows, cols] = change
        first = change.astype(bf16)
        left = change - first.astype(f32)
        second = left.astype(bf16)
        third = (left - second.astype(f32)).astype(bf16)
        side = bucket_side(table, head)
        for k, plane in enumerate((first, second, third)):
            start = pl.multiple_of(k * wide + side * HD, HD)
            split[table[head], :, pl.ds(start, HD)] = plane

    for bucket in range(parts):
        planes = split[bucket]
        one = planes[:, :wide]
        two = planes[:, wide : 2 * wide]
        mixed = dot_t(one, planes)
        rough = mixed[:, :wide] + dot_t(two, two)
        rough = rough + 2.0 * (mixed[:, wide : 2 * wide] + mixed[:, 2 * wide :])

        @pl.when(step == 0)
        def _():
            total[bucket] = rough

        @pl.when(step > 0)
        def _():
            total[bucket] = total[bucket] + rough

    @pl.when(step == pl.num_programs(0) - 1)
    def _():
        for bucket in range(parts):
            rough = total[bucket]
            mixed, side, diag = pack_symmetric(0.5 * (rough + rough.T))
            away = bucket ^ place[0]
            for k in range(parts):

                @pl.when(away == k)
                def _():
                    outs[k][0:HD, :] = mixed
                    outs[k][HD : 2 * HD, :] = side
                    outs[k][2 * HD : 2 * HD + 8, :] = diag


def local_grams(table, place, momentum, gradient, parts):
    layers, height, width = momentum.shape
    slots = width // HD
    tall = min(height, ROWS)
    block = pl.BlockSpec((layers, tall, width), lambda i, t, q: (0, i, 0))
    packed = (2 * HD + 8, HD)
    return pl.pallas_call(
        functools.partial(gram_kernel, parts=parts, slots=slots),
        grid_spec=pltpu.PrefetchScalarGridSpec(
            num_scalar_prefetch=2,
            grid=(height // tall,),
            in_specs=[block, block],
            out_specs=[block, pl.BlockSpec(memory_space=pltpu.VMEM)]
            + [pl.BlockSpec(packed, lambda i, t, q: (0, 0))] * parts,
            scratch_shapes=[
                pltpu.VMEM((parts, tall, 6 * HD), bf16),
                pltpu.VMEM((parts, 2 * HD, 2 * HD), f32),
            ],
        ),
        out_shape=[
            jax.ShapeDtypeStruct(momentum.shape, f32),
            pltpu.VMEM(momentum.shape, f32),
        ]
        + [jax.ShapeDtypeStruct(packed, f32)] * parts,
        compiler_params=pltpu.CompilerParams(vmem_limit_bytes=24 * MIB),
        name="grams",
    )(table, place, hbm(momentum), hbm(gradient))


def series_kernel(*refs, step_scale):
    *pieces, sums, out = refs
    packed = pieces[0][...]
    for ref in pieces[1:]:
        packed = packed + ref[...]
    total = unpack_symmetric(packed)
    rows, cols = grid_masks(total.shape[0])
    on_diag = rows == cols
    trace = jnp.sum(jnp.where(on_diag, total, 0.0), keepdims=True)
    scale = 1.0 / (jnp.sqrt(trace) + frob_epsilon)
    gram = total * (scale * scale)
    product = None
    for iteration in range(NS_ITERS):
        square = dot_full(gram, gram)
        factor = cube_coeff * gram + fifth_coeff * square
        factor = factor + jnp.where(on_diag, first_coeff, 0.0)
        product = factor if product is None else dot_full(product, factor)
        if iteration + 1 < NS_ITERS:
            gram = dot_full(dot_full(gram, factor), factor)
    store_packed(out, product * (scale * step_scale))
    high = pieces[0].shape[0]
    out[high : high + 8, :] = jnp.zeros((8, HD), f32)
    out[high : high + sums.shape[0], :] = sums[...]


def hbm(value):
    return pltpu.with_memory_space_constraint(value, pltpu.HBM)


def vmem(value):
    return pltpu.with_memory_space_constraint(value, pltpu.VMEM)


VM = pl.BlockSpec(memory_space=pltpu.VMEM)
SM = pl.BlockSpec(memory_space=pltpu.SMEM)


def series(pieces, sums, step_scale):
    high, wide = pieces[0].shape
    return pl.pallas_call(
        functools.partial(series_kernel, step_scale=step_scale),
        in_specs=[VM] * (len(pieces) + 1),
        out_specs=VM,
        out_shape=pltpu.VMEM((high + 8, wide), f32),
        compiler_params=pltpu.CompilerParams(vmem_limit_bytes=8 * MIB),
        name="series",
    )(*[vmem(p) for p in pieces], vmem(sums))


def apply_kernel(table, place, *refs, parts, slots, chunks):
    packed = refs[:parts]
    update, master, new_master = refs[parts : parts + 3]
    weights = refs[parts + 3 : parts + 3 + chunks]
    factors, fresh, sems = refs[-3:]
    layers, height, width = master.shape
    count = layers * slots
    wide = 2 * HD
    for k in range(parts):
        full = unpack_symmetric(packed[k][0 : 2 * HD + 8, :])
        one = full.astype(bf16)
        left = full - one.astype(f32)
        two = left.astype(bf16)
        three = (left - two.astype(f32)).astype(bf16)
        away = k ^ place[0]
        for spot, plane in enumerate((one, two, three, one, two, one)):
            factors[away, spot * wide : (spot + 1) * wide, :] = plane

    tall = min(height, ROWS)
    piece = width // chunks
    spots = []
    for place_of in range(count):
        head = head_of(table, place_of, count)
        spots.append((head // slots, pl.ds(pl.multiple_of(head % slots * HD, HD), HD)))
    copies = []
    for i in range(height // tall):
        rows = slice(i * tall, (i + 1) * tall)
        for bucket in range(parts):
            pair = [update[layer, rows, cols] for layer, cols in spots[2 * bucket : 2 * bucket + 2]]
            value = jnp.concatenate(pair, axis=1)
            one = value.astype(bf16)
            left = value - one.astype(f32)
            two = left.astype(bf16)
            three = (left - two.astype(f32)).astype(bf16)
            ortho = jnp.dot(
                jnp.concatenate([one, one, one, two, two, three], axis=1),
                factors[bucket],
                preferred_element_type=f32,
            )
            for side, (layer, cols) in enumerate(spots[2 * bucket : 2 * bucket + 2]):
                part = ortho[:, side * HD : (side + 1) * HD]
                fresh[layer, rows, cols] = master[layer, rows, cols] - part
        copies.append(
            pltpu.make_async_copy(fresh.at[:, rows, :], new_master.at[:, rows, :], sems.at[i])
        )
        copies[-1].start()
        for c in range(chunks):
            weights[c][rows, :] = fresh[0, rows, c * piece : (c + 1) * piece].astype(bf16)
    for copy in copies:
        copy.wait()


def apply_update(table, place, packed, update, master, chunks):
    layers, height, width = master.shape
    parts = len(packed)
    piece = (height, width // chunks)
    return pl.pallas_call(
        functools.partial(apply_kernel, parts=parts, slots=width // HD, chunks=chunks),
        in_specs=[SM, SM] + [VM] * (parts + 2),
        out_specs=[pl.BlockSpec(memory_space=pl.ANY)] + [VM] * chunks,
        scratch_shapes=[
            pltpu.VMEM((parts, 12 * HD, 2 * HD), bf16),
            pltpu.VMEM(master.shape, f32),
            pltpu.SemaphoreType.DMA((height // min(height, ROWS),)),
        ],
        out_shape=[jax.ShapeDtypeStruct(master.shape, f32)] + [pltpu.VMEM(piece, bf16)] * chunks,
        compiler_params=pltpu.CompilerParams(vmem_limit_bytes=16 * MIB),
        name="apply",
    )(table, place, *[vmem(p) for p in packed], vmem(update), vmem(master))


def norm_kernel(place, *refs, parts, features):
    halves = refs[: 2 * parts]
    packed = refs[2 * parts : 3 * parts]
    gain, out = refs[3 * parts :]
    height, width = halves[0].shape
    high = packed[0].shape[0] - 8
    for k in range(parts):
        inverse = lax.rsqrt(packed[k][high : high + 8, :] / features + rms_epsilon)
        away = k ^ place[0] ^ place[1]
        for side in range(2):
            for low in range(0, height, HD):
                spot = (side * height + low) // HD
                column = jnp.broadcast_to(inverse[spot : spot + 1, :], (HD, HD)).T
                for i in range(parts):

                    @pl.when(away == i)
                    def _():
                        for left in range(0, width, HD):
                            cols = slice(left, left + HD)
                            values = halves[2 * i + side][low : low + HD, cols].astype(f32)
                            out[k, spot * HD : (spot + 1) * HD, cols] = (
                                values * column * gain[:, cols]
                            ).astype(bf16)


def normalise(place, halves, packed, gain, features):
    parts = len(packed)
    height, width = halves[0].shape
    return pl.pallas_call(
        functools.partial(norm_kernel, parts=parts, features=features),
        in_specs=[SM] + [VM] * (3 * parts + 1),
        out_specs=VM,
        out_shape=pltpu.VMEM((parts, 2 * height, width), bf16),
        compiler_params=pltpu.CompilerParams(vmem_limit_bytes=8 * MIB),
        name="normalise",
    )(place, *[vmem(h) for h in halves], *[vmem(p) for p in packed], vmem(gain))


def project_kernel(place, normed, *refs, members, parts):
    weights = refs[:members]
    outs = refs[members : members + parts]
    whole = refs[-1]
    height = weights[0].shape[0]
    for k in range(members):
        start = pl.multiple_of((k ^ place[2]) * height, height)
        whole[pl.ds(start, height), :] = weights[k][...]
    for m in range(parts):
        outs[m][...] = jnp.dot(normed[m], whole[...], preferred_element_type=f32)


def project(place, normed, weights):
    parts, height, width = normed.shape
    cols = weights[0].shape[1]
    return pl.pallas_call(
        functools.partial(project_kernel, members=len(weights), parts=parts),
        in_specs=[SM] + [VM] * (1 + len(weights)),
        out_specs=[VM] * parts,
        out_shape=[pltpu.VMEM((height, cols), f32)] * parts,
        scratch_shapes=[pltpu.VMEM((width, cols), bf16)],
        compiler_params=pltpu.CompilerParams(vmem_limit_bytes=8 * MIB),
        name="project",
    )(place, vmem(normed), *[vmem(w) for w in weights])


def after(value, other):
    return lax.optimization_barrier((value, other))[0]


def per_device(master, momentum, gradient, bucket_table, tokens, norm_gain, *, dp, tp):
    layers, height, width = master.shape
    share = tokens.shape[1]
    features = norm_gain.shape[0]
    count = bucket_table.shape[1]
    parts = tp
    members = dp // parts
    assert count // 2 == parts and share * tp == features and height * dp == features
    mine = lax.axis_index("dp")
    column = lax.axis_index("tensor")
    row = mine // members
    place = jnp.stack([row, column, mine % members]).astype(jnp.int32)
    table = bucket_table[0]

    def swap_dp(value, bits):
        return lax.ppermute(value, "dp", [(i, i ^ bits) for i in range(dp)])

    def swap_tensor(value, bits):
        return lax.ppermute(value, "tensor", [(i, i ^ bits) for i in range(tp)])

    half = tokens.shape[0] // 2
    flips = (0, tp // 2)
    near = lax.slice_in_dim(tokens, 0, half, axis=0)
    far = swap_tensor(lax.slice_in_dim(tokens, half, 2 * half, axis=0), tp // 2)

    def turn(value, flip):
        pairs = []
        for q in range(parts):
            for r in range(members):
                for j in range(tp):
                    target = ((j ^ flip) * members + r) * tp + (q ^ flip)
                    pairs.append(((q * members + r) * tp + j, target))
        return lax.ppermute(value, ("dp", "tensor"), pairs)

    new_momentum, update, *grams = local_grams(table, place, momentum, gradient, parts)

    local_f = tokens.astype(f32)
    sums = jnp.sum(local_f * local_f, axis=1)
    bits = tp // 2
    while bits:
        sums = sums + swap_tensor(sums, bits)
        bits //= 2

    sent = [turn(after(value, grams[0]), flip) for value, flip in zip((near, far), flips)]
    total = grams[0]
    for k in range(1, parts):
        total = total + swap_dp(grams[k], k * members)
    pieces = [total]
    bits = 1
    while bits < members:
        pieces = [sum(pieces), swap_dp(sum(pieces), bits)]
        bits *= 2
    step_scale = learn_rate * math.sqrt(max(1.0, features / (2.0 * HD)))
    own = series(pieces, sums.reshape(-1, HD), step_scale)

    held = {(0, 0): after(sent[0], own), (1, tp // 2): after(sent[1], own)}
    bits = tp // 2
    while bits:
        fresh = {}
        for (side, offset), value in held.items():
            fresh[(side, offset ^ bits)] = swap_tensor(value, bits)
        held.update(fresh)
        bits //= 2
    halves = [held[(side, offset)] for offset in range(parts) for side in range(2)]
    packed = [own] + [swap_dp(own, k * members) for k in range(1, parts)]
    new_master, *weights = apply_update(table, place, packed, update, master, CHUNKS)
    gain = lax.dynamic_slice_in_dim(norm_gain, row * share, share, 0)[None, :]
    normed = normalise(place, halves, packed, gain, features)

    results = []
    for piece in weights:
        gathered = [piece] + [swap_dp(piece, k) for k in range(1, members)]
        partial = project(place, normed, gathered)
        result = partial[0]
        for k in range(1, parts):
            result = result + swap_dp(partial[k], k * members)
        results.append(result.astype(bf16))
    return (new_master, new_momentum, jnp.concatenate(results, axis=1))


def solution(mesh):
    placed = (
        P(None, "dp", "tensor"),
        P(None, "dp", "tensor"),
        P(None, "dp", "tensor"),
        P("tensor", None),
        P("dp", "tensor"),
        P(),
    )
    return jax.shard_map(
        functools.partial(per_device, dp=mesh.shape["dp"], tp=mesh.shape["tensor"]),
        mesh=mesh,
        in_specs=placed,
        out_specs=(P(None, "dp", "tensor"), P(None, "dp", "tensor"), P("dp", "tensor")),
        check_vma=False,
    )
```

```python
import functools
import math

import jax
import jax.numpy as jnp
from jax import lax
from jax.experimental import pallas as pl
from jax.experimental.pallas import tpu as pltpu
from jax.sharding import PartitionSpec as P


HD = 128
NS_ITERS = 3

beta_momentum = 0.95
learn_rate = 0.05
first_coeff = 3.4445
cube_coeff = -4.775
fifth_coeff = 2.0315
frob_epsilon = 1e-07
rms_epsilon = 1e-05

CHUNKS = 2
ROWS = 256
MIB = 1 << 20
CODE_ROWS = 16
CODE_BITS = 14.9
LEAST = 2.0**-100

bf16 = jnp.bfloat16
f32 = jnp.float32
HIGHEST = lax.Precision.HIGHEST


def head_of(table, place, count):
    bucket = place // 2
    lower = jnp.int32(0)
    upper = jnp.int32(0)
    for i in range(count):
        j = count - 1 - i
        lower = jnp.where(table[j] == bucket, j, lower)
        upper = jnp.where(table[i] == bucket, i, upper)
    return jnp.where(place % 2 == 0, lower, upper)


def grid_masks(size):
    rows = lax.broadcasted_iota(jnp.int32, (size, size), 0)
    cols = lax.broadcasted_iota(jnp.int32, (size, size), 1)
    return rows, cols


def pack_symmetric(full):
    half = full.shape[0] // 2
    rows, cols = grid_masks(half)
    low = full[half:, half:]
    mixed = jnp.where(rows <= cols, full[:half, :half], low)
    diag = jnp.sum(jnp.where(rows == cols, low, 0.0), axis=0, keepdims=True)
    return mixed, full[:half, half:], jnp.broadcast_to(diag, (8, half))


def unpack_symmetric(packed):
    half = packed.shape[1]
    mixed = packed[:half]
    side = packed[half : 2 * half]
    diag = packed[2 * half : 2 * half + 1]
    rows, cols = grid_masks(half)
    turned = mixed.T
    first = jnp.where(rows <= cols, mixed, turned)
    low = jnp.where(rows > cols, mixed, jnp.where(rows == cols, diag, turned))
    return jnp.concatenate(
        [
            jnp.concatenate([first, side], axis=1),
            jnp.concatenate([side.T, low], axis=1),
        ],
        axis=0,
    )


def store_packed(ref, full):
    half = full.shape[0] // 2
    mixed, side, diag = pack_symmetric(full)
    ref[0:half, :] = mixed
    ref[half : 2 * half, :] = side
    ref[2 * half : 2 * half + 8, :] = diag


def dot_t(a, b):
    return lax.dot_general(a, b, (((0,), (0,)), ((), ())), preferred_element_type=f32)


def dot_full(a, b):
    return lax.dot_general(
        a, b, (((1,), (0,)), ((), ())), precision=HIGHEST, preferred_element_type=f32
    )


def bucket_side(table, head):
    side = jnp.int32(0)
    for i in range(head):
        side = jnp.where(table[i] == table[head], 1, side)
    return side


def gram_kernel(table, place, momentum, gradient, new_momentum, update, *rest, parts, slots):
    outs = rest[:parts]
    split, total = rest[parts:]
    step = pl.program_id(0)
    layers, height, _ = momentum.shape
    wide = 2 * HD
    rows = pl.ds(pl.multiple_of(step * height, height), height)
    for head in range(layers * slots):
        layer = head // slots
        cols = slice((head % slots) * HD, (head % slots + 1) * HD)
        slope = gradient[layer, :, cols]
        fresh = beta_momentum * momentum[layer, :, cols] + slope
        new_momentum[layer, :, cols] = fresh
        change = slope + beta_momentum * fresh
        update[layer, rows, cols] = change
        first = change.astype(bf16)
        left = change - first.astype(f32)
        second = left.astype(bf16)
        third = (left - second.astype(f32)).astype(bf16)
        side = bucket_side(table, head)
        for k, plane in enumerate((first, second, third)):
            start = pl.multiple_of(k * wide + side * HD, HD)
            split[table[head], :, pl.ds(start, HD)] = plane

    for bucket in range(parts):
        planes = split[bucket]
        one = planes[:, :wide]
        two = planes[:, wide : 2 * wide]
        mixed = dot_t(one, planes)
        rough = mixed[:, :wide] + dot_t(two, two)
        rough = rough + 2.0 * (mixed[:, wide : 2 * wide] + mixed[:, 2 * wide :])

        @pl.when(step == 0)
        def _():
            total[bucket] = rough

        @pl.when(step > 0)
        def _():
            total[bucket] = total[bucket] + rough

    @pl.when(step == pl.num_programs(0) - 1)
    def _():
        for bucket in range(parts):
            rough = total[bucket]
            mixed, side, diag = pack_symmetric(0.5 * (rough + rough.T))
            away = bucket ^ place[0]
            for k in range(parts):

                @pl.when(away == k)
                def _():
                    outs[k][0:HD, :] = mixed
                    outs[k][HD : 2 * HD, :] = side
                    outs[k][2 * HD : 2 * HD + 8, :] = diag


def local_grams(table, place, momentum, gradient, parts):
    layers, height, width = momentum.shape
    slots = width // HD
    tall = min(height, ROWS)
    block = pl.BlockSpec((layers, tall, width), lambda i, t, q: (0, i, 0))
    packed = (2 * HD + 8, HD)
    return pl.pallas_call(
        functools.partial(gram_kernel, parts=parts, slots=slots),
        grid_spec=pltpu.PrefetchScalarGridSpec(
            num_scalar_prefetch=2,
            grid=(height // tall,),
            in_specs=[block, block],
            out_specs=[block, pl.BlockSpec(memory_space=pltpu.VMEM)]
            + [pl.BlockSpec(packed, lambda i, t, q: (0, 0))] * parts,
            scratch_shapes=[
                pltpu.VMEM((parts, tall, 6 * HD), bf16),
                pltpu.VMEM((parts, 2 * HD, 2 * HD), f32),
            ],
        ),
        out_shape=[
            jax.ShapeDtypeStruct(momentum.shape, f32),
            pltpu.VMEM(momentum.shape, f32),
        ]
        + [jax.ShapeDtypeStruct(packed, f32)] * parts,
        compiler_params=pltpu.CompilerParams(vmem_limit_bytes=24 * MIB),
        name="grams",
    )(table, place, hbm(momentum), hbm(gradient))


def series_kernel(*refs, step_scale):
    *pieces, sums, out = refs
    packed = pieces[0][...]
    for ref in pieces[1:]:
        packed = packed + ref[...]
    total = unpack_symmetric(packed)
    rows, cols = grid_masks(total.shape[0])
    on_diag = rows == cols
    trace = jnp.sum(jnp.where(on_diag, total, 0.0), keepdims=True)
    scale = 1.0 / (jnp.sqrt(trace) + frob_epsilon)
    gram = total * (scale * scale)
    product = None
    for iteration in range(NS_ITERS):
        square = dot_full(gram, gram)
        factor = cube_coeff * gram + fifth_coeff * square
        factor = factor + jnp.where(on_diag, first_coeff, 0.0)
        product = factor if product is None else dot_full(product, factor)
        if iteration + 1 < NS_ITERS:
            gram = dot_full(dot_full(gram, factor), factor)
    store_packed(out, product * (scale * step_scale))
    high = pieces[0].shape[0]
    out[high : high + 8, :] = jnp.zeros((8, HD), f32)
    out[high : high + sums.shape[0], :] = sums[...]


def hbm(value):
    return pltpu.with_memory_space_constraint(value, pltpu.HBM)


def vmem(value):
    return pltpu.with_memory_space_constraint(value, pltpu.VMEM)


VM = pl.BlockSpec(memory_space=pltpu.VMEM)
SM = pl.BlockSpec(memory_space=pltpu.SMEM)


def series(pieces, sums, step_scale):
    high, wide = pieces[0].shape
    return pl.pallas_call(
        functools.partial(series_kernel, step_scale=step_scale),
        in_specs=[VM] * (len(pieces) + 1),
        out_specs=VM,
        out_shape=pltpu.VMEM((high + 8, wide), f32),
        compiler_params=pltpu.CompilerParams(vmem_limit_bytes=8 * MIB),
        name="series",
    )(*[vmem(p) for p in pieces], vmem(sums))


def split_three(value):
    one = value.astype(bf16)
    left = value - one.astype(f32)
    two = left.astype(bf16)
    return one, two, (left - two.astype(f32)).astype(bf16)


def head_pair(update, rows, spots):
    pair = [update[layer, rows, cols] for layer, cols in spots]
    one, two, three = split_three(jnp.concatenate(pair, axis=1))
    return jnp.concatenate([one, one, one, two, two, three], axis=1)


def head_spots(table, bucket, slots, count):
    spots = []
    for side in range(2):
        head = head_of(table, 2 * bucket + side, count)
        spots.append((head // slots, pl.ds(pl.multiple_of(head % slots * HD, HD), HD)))
    return spots


def lead_kernel(table, place, *refs, parts, slots, heads):
    packed = refs[:parts]
    update, master, weights, factors = refs[parts:]
    layers, height, _ = master.shape
    wide = 2 * HD
    for k in range(parts):
        planes = split_three(unpack_symmetric(packed[k][0 : 2 * HD + 8, :]))
        away = k ^ place[0]
        for spot, plane in enumerate((0, 1, 2, 0, 1, 0)):
            factors[away, spot * wide : (spot + 1) * wide, :] = planes[plane]

    tall = min(height, ROWS)
    for head in range(heads):
        bucket = table[head]
        start = pl.multiple_of(bucket_side(table, head) * HD, HD)
        factor = factors[bucket, :, pl.ds(start, HD)]
        spots = head_spots(table, bucket, slots, layers * slots)
        cols = slice(head * HD, (head + 1) * HD)
        for low in range(0, height, tall):
            rows = slice(low, low + tall)
            value = head_pair(update, rows, spots)
            ortho = jnp.dot(value, factor, preferred_element_type=f32)
            weights[rows, cols] = (master[0, rows, cols] - ortho).astype(bf16)


def lead_weights(table, place, packed, update, master, chunks):
    _, height, width = master.shape
    parts = len(packed)
    slots = width // HD
    return pl.pallas_call(
        functools.partial(lead_kernel, parts=parts, slots=slots, heads=slots // chunks),
        in_specs=[SM, SM] + [VM] * (parts + 2),
        out_specs=[VM, VM],
        out_shape=[
            pltpu.VMEM((height, width // chunks), bf16),
            pltpu.VMEM((parts, 12 * HD, 2 * HD), bf16),
        ],
        compiler_params=pltpu.CompilerParams(vmem_limit_bytes=12 * MIB),
        name="lead",
    )(table, place, *[vmem(p) for p in packed], vmem(update), vmem(master))


def apply_kernel(table, factors, update, master, new_master, *refs, chunks):
    weights = refs[: chunks - 1]
    fresh, sems = refs[chunks - 1 :]
    layers, height, width = master.shape
    slots = width // HD
    tall = min(height, ROWS)
    piece = width // chunks
    parts = factors.shape[0]
    spots = [head_spots(table, bucket, slots, layers * slots) for bucket in range(parts)]
    copies = []
    for i in range(height // tall):
        rows = slice(i * tall, (i + 1) * tall)
        for bucket in range(parts):
            value = head_pair(update, rows, spots[bucket])
            ortho = jnp.dot(value, factors[bucket], preferred_element_type=f32)
            for side, (layer, cols) in enumerate(spots[bucket]):
                part = ortho[:, side * HD : (side + 1) * HD]
                fresh[layer, rows, cols] = master[layer, rows, cols] - part
        copies.append(
            pltpu.make_async_copy(fresh.at[:, rows, :], new_master.at[:, rows, :], sems.at[i])
        )
        copies[-1].start()
        for c in range(1, chunks):
            cols = slice(c * piece, (c + 1) * piece)
            weights[c - 1][rows, :] = fresh[0, rows, cols].astype(bf16)
    for copy in copies:
        copy.wait()


def apply_update(table, factors, update, master, chunks):
    _, height, width = master.shape
    return pl.pallas_call(
        functools.partial(apply_kernel, chunks=chunks),
        in_specs=[SM] + [VM] * 3,
        out_specs=[pl.BlockSpec(memory_space=pl.ANY)] + [VM] * (chunks - 1),
        scratch_shapes=[
            pltpu.VMEM(master.shape, f32),
            pltpu.SemaphoreType.DMA((height // min(height, ROWS),)),
        ],
        out_shape=[jax.ShapeDtypeStruct(master.shape, f32)]
        + [pltpu.VMEM((height, width // chunks), bf16)] * (chunks - 1),
        compiler_params=pltpu.CompilerParams(vmem_limit_bytes=12 * MIB),
        name="apply",
    )(table, vmem(factors), vmem(update), vmem(master))


def norm_kernel(place, *refs, parts, features):
    halves = refs[: 2 * parts]
    packed = refs[2 * parts : 3 * parts]
    gain, out = refs[3 * parts :]
    height, width = halves[0].shape
    high = packed[0].shape[0] - 8
    for k in range(parts):
        inverse = lax.rsqrt(packed[k][high : high + 8, :] / features + rms_epsilon)
        away = k ^ place[0] ^ place[1]
        for side in range(2):
            for low in range(0, height, HD):
                spot = (side * height + low) // HD
                column = jnp.broadcast_to(inverse[spot : spot + 1, :], (HD, HD)).T
                for i in range(parts):

                    @pl.when(away == i)
                    def _():
                        for left in range(0, width, HD):
                            cols = slice(left, left + HD)
                            values = halves[2 * i + side][low : low + HD, cols].astype(f32)
                            out[k, spot * HD : (spot + 1) * HD, cols] = (
                                values * column * gain[:, cols]
                            ).astype(bf16)


def normalise(place, halves, packed, gain, features):
    parts = len(packed)
    height, width = halves[0].shape
    return pl.pallas_call(
        functools.partial(norm_kernel, parts=parts, features=features),
        in_specs=[SM] + [VM] * (3 * parts + 1),
        out_specs=VM,
        out_shape=pltpu.VMEM((parts, 2 * height, width), bf16),
        compiler_params=pltpu.CompilerParams(vmem_limit_bytes=8 * MIB),
        name="normalise",
    )(place, *[vmem(h) for h in halves], *[vmem(p) for p in packed], vmem(gain))


def project_kernel(place, normed, *refs, members, parts):
    weights = refs[:members]
    outs = refs[members : members + parts]
    whole = refs[-1]
    height = weights[0].shape[0]
    for k in range(members):
        start = pl.multiple_of((k ^ place[2]) * height, height)
        whole[pl.ds(start, height), :] = weights[k][...]
    for m in range(parts):
        part = jnp.dot(normed[m], whole[...], preferred_element_type=f32)
        if m == 0:
            outs[m][...] = part
        else:
            encode(outs[m], part)


def encode(out, value):
    height = value.shape[0]
    top = jnp.max(jnp.abs(value), axis=0, keepdims=True)
    power = jnp.ceil(jnp.log2(jnp.maximum(top, LEAST)) - CODE_BITS)
    code = jnp.round(value * jnp.exp2(-power))
    out[0:height, :] = code.astype(jnp.int32).astype(jnp.int16)
    tail = jnp.broadcast_to(power, (CODE_ROWS, value.shape[1]))
    out[height : height + CODE_ROWS, :] = tail.astype(jnp.int32).astype(jnp.int16)


def finish_kernel(*refs, chunks, parts):
    out = refs[-1]
    for c in range(chunks):
        own, *codes = refs[c * parts : (c + 1) * parts]
        height, width = own.shape
        total = own[...]
        for code in codes:
            power = code[height : height + CODE_ROWS, :].astype(jnp.int32).astype(f32)
            value = code[0:height, :].astype(jnp.int32).astype(f32)
            total = total + value * jnp.exp2(power[0:1, :])
        out[:, c * width : (c + 1) * width] = total.astype(bf16)


def finish(pieces):
    chunks = len(pieces)
    parts = len(pieces[0])
    height, width = pieces[0][0].shape
    return pl.pallas_call(
        functools.partial(finish_kernel, chunks=chunks, parts=parts),
        in_specs=[VM] * (chunks * parts),
        out_shape=jax.ShapeDtypeStruct((height, chunks * width), bf16),
        compiler_params=pltpu.CompilerParams(vmem_limit_bytes=8 * MIB),
        name="finish",
    )(*[vmem(p) for piece in pieces for p in piece])


def project(place, normed, weights):
    parts, height, width = normed.shape
    cols = weights[0].shape[1]
    code = pltpu.VMEM((height + CODE_ROWS, cols), jnp.int16)
    return pl.pallas_call(
        functools.partial(project_kernel, members=len(weights), parts=parts),
        in_specs=[SM] + [VM] * (1 + len(weights)),
        out_specs=[VM] * parts,
        out_shape=[pltpu.VMEM((height, cols), f32)] + [code] * (parts - 1),
        scratch_shapes=[pltpu.VMEM((width, cols), bf16)],
        compiler_params=pltpu.CompilerParams(vmem_limit_bytes=8 * MIB),
        name="project",
    )(place, vmem(normed), *[vmem(w) for w in weights])


def after(value, other):
    return lax.optimization_barrier((value, other))[0]


def per_device(master, momentum, gradient, bucket_table, tokens, norm_gain, *, dp, tp):
    _, height, _ = master.shape
    share = tokens.shape[1]
    features = norm_gain.shape[0]
    count = bucket_table.shape[1]
    parts = tp
    members = dp // parts
    assert count // 2 == parts and share * tp == features and height * dp == features
    mine = lax.axis_index("dp")
    column = lax.axis_index("tensor")
    row = mine // members
    place = jnp.stack([row, column, mine % members]).astype(jnp.int32)
    table = bucket_table[0]

    def swap_dp(value, bits):
        return lax.ppermute(value, "dp", [(i, i ^ bits) for i in range(dp)])

    def swap_tensor(value, bits):
        return lax.ppermute(value, "tensor", [(i, i ^ bits) for i in range(tp)])

    half = tokens.shape[0] // 2
    flips = (0, tp // 2)
    near = lax.slice_in_dim(tokens, 0, half, axis=0)
    far = swap_tensor(lax.slice_in_dim(tokens, half, 2 * half, axis=0), tp // 2)

    def turn(value, flip):
        pairs = []
        for q in range(parts):
            for r in range(members):
                for j in range(tp):
                    target = ((j ^ flip) * members + r) * tp + (q ^ flip)
                    pairs.append(((q * members + r) * tp + j, target))
        return lax.ppermute(value, ("dp", "tensor"), pairs)

    new_momentum, update, *grams = local_grams(table, place, momentum, gradient, parts)

    local_f = tokens.astype(f32)
    sums = jnp.sum(local_f * local_f, axis=1)
    bits = tp // 2
    while bits:
        sums = sums + swap_tensor(sums, bits)
        bits //= 2

    sent = [turn(after(value, grams[0]), flip) for value, flip in zip((near, far), flips)]
    total = grams[0]
    for k in range(1, parts):
        total = total + swap_dp(grams[k], k * members)
    pieces = [total]
    bits = 1
    while bits < members:
        pieces = [sum(pieces), swap_dp(sum(pieces), bits)]
        bits *= 2
    step_scale = learn_rate * math.sqrt(max(1.0, features / (2.0 * HD)))
    own = series(pieces, sums.reshape(-1, HD), step_scale)

    packed = [own] + [swap_dp(own, k * members) for k in range(1, parts)]
    lead, factors = lead_weights(table, place, packed, update, master, CHUNKS)
    new_master, *others = apply_update(table, factors, update, master, CHUNKS)

    held = {(0, 0): after(sent[0], own), (1, tp // 2): after(sent[1], own)}
    bits = tp // 2
    while bits:
        fresh = {}
        for (side, offset), value in held.items():
            if bits < tp // 2:
                value = after(value, others[0] if others else lead)
            fresh[(side, offset ^ bits)] = swap_tensor(value, bits)
        held.update(fresh)
        bits //= 2
    halves = [held[(side, offset)] for offset in range(parts) for side in range(2)]
    gain = lax.dynamic_slice_in_dim(norm_gain, row * share, share, 0)[None, :]
    normed = normalise(place, halves, packed, gain, features)

    pieces = []
    for piece in [lead] + others:
        gathered = [piece] + [swap_dp(piece, k) for k in range(1, members)]
        partial = project(place, normed, gathered)
        sums_of = [swap_dp(partial[k], k * members) for k in range(1, parts)]
        pieces.append([partial[0]] + sums_of)
    return (new_master, new_momentum, finish(pieces))


def solution(mesh):
    placed = (
        P(None, "dp", "tensor"),
        P(None, "dp", "tensor"),
        P(None, "dp", "tensor"),
        P("tensor", None),
        P("dp", "tensor"),
        P(),
    )

    def step(*args):
        return per_device(*args, dp=mesh.shape["dp"], tp=mesh.shape["tensor"])

    return jax.shard_map(
        step,
        mesh=mesh,
        in_specs=placed,
        out_specs=(P(None, "dp", "tensor"), P(None, "dp", "tensor"), P("dp", "tensor")),
        check_vma=False,
    )
```

```python
import functools
import math

import jax
import jax.numpy as jnp
from jax import lax
from jax.experimental import pallas as pl
from jax.experimental.pallas import tpu as pltpu
from jax.sharding import PartitionSpec as P


HD = 128
NS_ITERS = 3

beta_momentum = 0.95
learn_rate = 0.05
first_coeff = 3.4445
cube_coeff = -4.775
fifth_coeff = 2.0315
frob_epsilon = 1e-07
rms_epsilon = 1e-05

CHUNKS = 2
ROWS = 256
MIB = 1 << 20
CODE_ROWS = 16
CODE_BITS = 14.9
LEAST = 2.0**-100

bf16 = jnp.bfloat16
f32 = jnp.float32
HIGHEST = lax.Precision.HIGHEST
VM = pl.BlockSpec(memory_space=pltpu.VMEM)
SM = pl.BlockSpec(memory_space=pltpu.SMEM)


def head_of(table, place, count):
    bucket = place // 2
    lower = jnp.int32(0)
    upper = jnp.int32(0)
    for i in range(count):
        j = count - 1 - i
        lower = jnp.where(table[0, j] == bucket, j, lower)
        upper = jnp.where(table[0, i] == bucket, i, upper)
    return jnp.where(place % 2 == 0, lower, upper)


def grid_masks(size):
    rows = lax.broadcasted_iota(jnp.int32, (size, size), 0)
    cols = lax.broadcasted_iota(jnp.int32, (size, size), 1)
    return rows, cols


def pack_symmetric(full):
    half = full.shape[0] // 2
    rows, cols = grid_masks(half)
    low = full[half:, half:]
    mixed = jnp.where(rows <= cols, full[:half, :half], low)
    diag = jnp.sum(jnp.where(rows == cols, low, 0.0), axis=0, keepdims=True)
    return mixed, full[:half, half:], jnp.broadcast_to(diag, (8, half))


def unpack_symmetric(packed):
    half = packed.shape[1]
    mixed = packed[:half]
    side = packed[half : 2 * half]
    diag = packed[2 * half : 2 * half + 1]
    rows, cols = grid_masks(half)
    turned = mixed.T
    first = jnp.where(rows <= cols, mixed, turned)
    low = jnp.where(rows > cols, mixed, jnp.where(rows == cols, diag, turned))
    return jnp.concatenate(
        [
            jnp.concatenate([first, side], axis=1),
            jnp.concatenate([side.T, low], axis=1),
        ],
        axis=0,
    )


def store_packed(ref, full):
    half = full.shape[0] // 2
    mixed, side, diag = pack_symmetric(full)
    ref[0:half, :] = mixed
    ref[half : 2 * half, :] = side
    ref[2 * half : 2 * half + 8, :] = diag


def dot_t(a, b):
    return lax.dot_general(a, b, (((0,), (0,)), ((), ())), preferred_element_type=f32)


def dot_full(a, b):
    return lax.dot_general(
        a, b, (((1,), (0,)), ((), ())), precision=HIGHEST, preferred_element_type=f32
    )


def bucket_side(table, head):
    side = jnp.int32(0)
    for i in range(head):
        side = jnp.where(table[0, i] == table[0, head], 1, side)
    return side


def gram_kernel(table, place, momentum, gradient, new_momentum, update, *rest, parts):
    outs = rest[:parts]
    held, slopes, split, total, arrive, leave = rest[parts:]
    layers, height, width = update.shape
    slots = width // HD
    tall = split.shape[1]
    wide = 2 * HD
    blocks = [slice(low, low + tall) for low in range(0, height, tall)]
    loads = []
    for i, rows in enumerate(blocks):
        loads.append(
            (
                pltpu.make_async_copy(momentum.at[:, rows, :], held.at[:, rows, :], arrive.at[0, i]),
                pltpu.make_async_copy(gradient.at[:, rows, :], slopes.at[:, rows, :], arrive.at[1, i]),
            )
        )
        for load in loads[-1]:
            load.start()
    stores = []
    for i, rows in enumerate(blocks):
        for load in loads[i]:
            load.wait()
        for head in range(layers * slots):
            layer = head // slots
            cols = slice((head % slots) * HD, (head % slots + 1) * HD)
            slope = slopes[layer, rows, cols]
            fresh = beta_momentum * held[layer, rows, cols] + slope
            held[layer, rows, cols] = fresh
            change = slope + beta_momentum * fresh
            update[layer, rows, cols] = change
            side = bucket_side(table, head)
            for k, plane in enumerate(split_three(change)):
                start = pl.multiple_of(k * wide + side * HD, HD)
                split[table[0, head], :, pl.ds(start, HD)] = plane
        stores.append(
            pltpu.make_async_copy(held.at[:, rows, :], new_momentum.at[:, rows, :], leave.at[i])
        )
        stores[-1].start()
        for bucket in range(parts):
            planes = split[bucket]
            two = planes[:, wide : 2 * wide]
            mixed = dot_t(planes[:, :wide], planes)
            rough = mixed[:, :wide] + dot_t(two, two)
            rough = rough + 2.0 * (mixed[:, wide : 2 * wide] + mixed[:, 2 * wide :])
            if i > 0:
                rough = total[bucket] + rough
            if i + 1 < len(blocks):
                total[bucket] = rough
                continue
            mixed, side, diag = pack_symmetric(0.5 * (rough + rough.T))
            away = bucket ^ place[0]
            for k in range(parts):

                @pl.when(away == k)
                def _():
                    outs[k][0:HD, :] = mixed
                    outs[k][HD : 2 * HD, :] = side
                    outs[k][2 * HD : 2 * HD + 8, :] = diag

    for store in stores:
        store.wait()


def local_grams(table, place, momentum, gradient, parts):
    shape = momentum.shape
    tall = min(shape[1], ROWS)
    blocks = shape[1] // tall
    packed = (2 * HD + 8, HD)
    anywhere = pl.BlockSpec(memory_space=pl.ANY)
    return pl.pallas_call(
        functools.partial(gram_kernel, parts=parts),
        in_specs=[SM, SM, anywhere, anywhere],
        out_specs=[anywhere] + [VM] * (parts + 1),
        scratch_shapes=[
            pltpu.VMEM(shape, f32),
            pltpu.VMEM(shape, f32),
            pltpu.VMEM((parts, tall, 6 * HD), bf16),
            pltpu.VMEM((parts, 2 * HD, 2 * HD), f32),
            pltpu.SemaphoreType.DMA((2, blocks)),
            pltpu.SemaphoreType.DMA((blocks,)),
        ],
        out_shape=[jax.ShapeDtypeStruct(shape, f32), pltpu.VMEM(shape, f32)]
        + [pltpu.VMEM(packed, f32)] * parts,
        compiler_params=pltpu.CompilerParams(vmem_limit_bytes=24 * MIB),
        name="grams",
    )(table, place, hbm(momentum), hbm(gradient))


def series_kernel(*refs, step_scale):
    *pieces, sums, out = refs
    packed = pieces[0][...]
    for ref in pieces[1:]:
        packed = packed + ref[...]
    total = unpack_symmetric(packed)
    rows, cols = grid_masks(total.shape[0])
    on_diag = rows == cols
    trace = jnp.sum(jnp.where(on_diag, total, 0.0), keepdims=True)
    scale = 1.0 / (jnp.sqrt(trace) + frob_epsilon)
    gram = total * (scale * scale)
    product = None
    for iteration in range(NS_ITERS):
        square = dot_full(gram, gram)
        factor = cube_coeff * gram + fifth_coeff * square
        factor = factor + jnp.where(on_diag, first_coeff, 0.0)
        product = factor if product is None else dot_full(product, factor)
        if iteration + 1 < NS_ITERS:
            gram = dot_full(dot_full(gram, factor), factor)
    store_packed(out, product * (scale * step_scale))
    high = pieces[0].shape[0]
    out[high : high + 8, :] = jnp.zeros((8, HD), f32)
    out[high : high + sums.shape[0], :] = sums[...]


def hbm(value):
    return pltpu.with_memory_space_constraint(value, pltpu.HBM)


def vmem(value):
    return pltpu.with_memory_space_constraint(value, pltpu.VMEM)


def series(pieces, sums, step_scale):
    high, wide = pieces[0].shape
    return pl.pallas_call(
        functools.partial(series_kernel, step_scale=step_scale),
        in_specs=[VM] * (len(pieces) + 1),
        out_specs=VM,
        out_shape=pltpu.VMEM((high + 8, wide), f32),
        compiler_params=pltpu.CompilerParams(vmem_limit_bytes=8 * MIB),
        name="series",
    )(*[vmem(p) for p in pieces], vmem(sums))


def split_three(value):
    one = value.astype(bf16)
    left = value - one.astype(f32)
    two = left.astype(bf16)
    return one, two, (left - two.astype(f32)).astype(bf16)


def head_pair(update, rows, spots):
    pair = [update[layer, rows, cols] for layer, cols in spots]
    one, two, three = split_three(jnp.concatenate(pair, axis=1))
    return jnp.concatenate([one, one, one, two, two, three], axis=1)


def head_spots(table, bucket, slots, count):
    spots = []
    for side in range(2):
        head = head_of(table, 2 * bucket + side, count)
        spots.append((head // slots, pl.ds(pl.multiple_of(head % slots * HD, HD), HD)))
    return spots


def lead_kernel(table, place, *refs, parts, slots, heads):
    packed = refs[:parts]
    update, master, weights, factors = refs[parts:]
    layers, height, _ = master.shape
    wide = 2 * HD
    for k in range(parts):
        planes = split_three(unpack_symmetric(packed[k][0 : 2 * HD + 8, :]))
        away = k ^ place[0]
        for spot, plane in enumerate((0, 1, 2, 0, 1, 0)):
            factors[away, spot * wide : (spot + 1) * wide, :] = planes[plane]

    tall = min(height, ROWS)
    for head in range(heads):
        bucket = table[0, head]
        start = pl.multiple_of(bucket_side(table, head) * HD, HD)
        factor = factors[bucket, :, pl.ds(start, HD)]
        spots = head_spots(table, bucket, slots, layers * slots)
        cols = slice(head * HD, (head + 1) * HD)
        for low in range(0, height, tall):
            rows = slice(low, low + tall)
            value = head_pair(update, rows, spots)
            ortho = jnp.dot(value, factor, preferred_element_type=f32)
            weights[rows, cols] = (master[0, rows, cols] - ortho).astype(bf16)


def lead_weights(table, place, packed, update, master, chunks):
    _, height, width = master.shape
    parts = len(packed)
    slots = width // HD
    return pl.pallas_call(
        functools.partial(lead_kernel, parts=parts, slots=slots, heads=slots // chunks),
        in_specs=[SM, SM] + [VM] * (parts + 2),
        out_specs=[VM, VM],
        out_shape=[
            pltpu.VMEM((height, width // chunks), bf16),
            pltpu.VMEM((parts, 12 * HD, 2 * HD), bf16),
        ],
        compiler_params=pltpu.CompilerParams(vmem_limit_bytes=12 * MIB),
        name="lead",
    )(table, place, *[vmem(p) for p in packed], vmem(update), vmem(master))


def apply_kernel(table, factors, update, master, new_master, *refs, chunks):
    weights = refs[: chunks - 1]
    fresh, sems = refs[chunks - 1 :]
    layers, height, width = master.shape
    slots = width // HD
    tall = min(height, ROWS)
    piece = width // chunks
    parts = factors.shape[0]
    spots = [head_spots(table, bucket, slots, layers * slots) for bucket in range(parts)]
    copies = []
    for i in range(height // tall):
        rows = slice(i * tall, (i + 1) * tall)
        for bucket in range(parts):
            value = head_pair(update, rows, spots[bucket])
            ortho = jnp.dot(value, factors[bucket], preferred_element_type=f32)
            for side, (layer, cols) in enumerate(spots[bucket]):
                part = ortho[:, side * HD : (side + 1) * HD]
                fresh[layer, rows, cols] = master[layer, rows, cols] - part
        copies.append(
            pltpu.make_async_copy(fresh.at[:, rows, :], new_master.at[:, rows, :], sems.at[i])
        )
        copies[-1].start()
        for c in range(1, chunks):
            cols = slice(c * piece, (c + 1) * piece)
            weights[c - 1][rows, :] = fresh[0, rows, cols].astype(bf16)
    for copy in copies:
        copy.wait()


def apply_update(table, factors, update, master, chunks):
    _, height, width = master.shape
    return pl.pallas_call(
        functools.partial(apply_kernel, chunks=chunks),
        in_specs=[SM] + [VM] * 3,
        out_specs=[pl.BlockSpec(memory_space=pl.ANY)] + [VM] * (chunks - 1),
        scratch_shapes=[
            pltpu.VMEM(master.shape, f32),
            pltpu.SemaphoreType.DMA((height // min(height, ROWS),)),
        ],
        out_shape=[jax.ShapeDtypeStruct(master.shape, f32)]
        + [pltpu.VMEM((height, width // chunks), bf16)] * (chunks - 1),
        compiler_params=pltpu.CompilerParams(vmem_limit_bytes=12 * MIB),
        name="apply",
    )(table, vmem(factors), vmem(update), vmem(master))


def norm_kernel(place, *refs, parts, base, features):
    pieces = refs[:parts]
    packed = refs[parts : 2 * parts]
    gain, out, sums = refs[2 * parts :]
    height, width = pieces[0].shape
    high = packed[0].shape[0] - 8
    for k in range(parts):
        sums[k] = lax.rsqrt(packed[k][high : high + 8, :] / features + rms_epsilon)
    for k in range(parts):
        away = k ^ place[0] ^ place[1]
        inverse = sums[away]
        for low in range(0, height, HD):
            spot = (base + low) // HD
            column = jnp.broadcast_to(inverse[spot : spot + 1, :], (HD, HD)).T
            for left in range(0, width, HD):
                cols = slice(left, left + HD)
                values = pieces[k][low : low + HD, cols].astype(f32)
                out[away, low : low + HD, cols] = (values * column * gain[:, cols]).astype(bf16)


def normalise(place, pieces, packed, gain, base, features):
    parts = len(packed)
    height, width = pieces[0].shape
    return pl.pallas_call(
        functools.partial(norm_kernel, parts=parts, base=base, features=features),
        in_specs=[SM] + [VM] * (2 * parts + 1),
        out_specs=VM,
        out_shape=pltpu.VMEM((parts, height, width), bf16),
        scratch_shapes=[pltpu.VMEM((parts, 8, HD), f32)],
        compiler_params=pltpu.CompilerParams(vmem_limit_bytes=8 * MIB),
        name="normalise",
    )(place, *[vmem(p) for p in pieces], *[vmem(p) for p in packed], vmem(gain))


def project_kernel(place, near, far, *refs, members, parts):
    weights = refs[:members]
    outs = refs[members : members + parts]
    whole = refs[-1]
    height = weights[0].shape[0]
    for k in range(members):
        start = pl.multiple_of((k ^ place[2]) * height, height)
        whole[pl.ds(start, height), :] = weights[k][...]
    for m in range(parts):
        both = [jnp.dot(half[m], whole[...], preferred_element_type=f32) for half in (near, far)]
        part = jnp.concatenate(both, axis=0)
        if m == 0:
            outs[m][...] = part
        else:
            encode(outs[m], part)


def encode(out, value):
    height = value.shape[0]
    top = jnp.max(jnp.abs(value), axis=0, keepdims=True)
    power = jnp.ceil(jnp.log2(jnp.maximum(top, LEAST)) - CODE_BITS)
    code = jnp.round(value * jnp.exp2(-power))
    out[0:height, :] = code.astype(jnp.int32).astype(jnp.int16)
    tail = jnp.broadcast_to(power, (CODE_ROWS, value.shape[1]))
    out[height : height + CODE_ROWS, :] = tail.astype(jnp.int32).astype(jnp.int16)


def finish_kernel(*refs, chunks, parts):
    out = refs[-1]
    for c in range(chunks):
        own, *codes = refs[c * parts : (c + 1) * parts]
        height, width = own.shape
        total = own[...]
        for code in codes:
            power = code[height : height + CODE_ROWS, :].astype(jnp.int32).astype(f32)
            value = code[0:height, :].astype(jnp.int32).astype(f32)
            total = total + value * jnp.exp2(power[0:1, :])
        out[:, c * width : (c + 1) * width] = total.astype(bf16)


def finish(pieces):
    chunks = len(pieces)
    parts = len(pieces[0])
    height, width = pieces[0][0].shape
    return pl.pallas_call(
        functools.partial(finish_kernel, chunks=chunks, parts=parts),
        in_specs=[VM] * (chunks * parts),
        out_shape=jax.ShapeDtypeStruct((height, chunks * width), bf16),
        compiler_params=pltpu.CompilerParams(vmem_limit_bytes=8 * MIB),
        name="finish",
    )(*[vmem(p) for piece in pieces for p in piece])


def project(place, near, far, weights):
    parts, height, width = near.shape
    height *= 2
    cols = weights[0].shape[1]
    code = pltpu.VMEM((height + CODE_ROWS, cols), jnp.int16)
    return pl.pallas_call(
        functools.partial(project_kernel, members=len(weights), parts=parts),
        in_specs=[SM] + [VM] * (2 + len(weights)),
        out_specs=[VM] * parts,
        out_shape=[pltpu.VMEM((height, cols), f32)] + [code] * (parts - 1),
        scratch_shapes=[pltpu.VMEM((width, cols), bf16)],
        compiler_params=pltpu.CompilerParams(vmem_limit_bytes=8 * MIB),
        name="project",
    )(place, vmem(near), vmem(far), *[vmem(w) for w in weights])


def after(value, other):
    return lax.optimization_barrier((value, other))[0]


def per_device(master, momentum, gradient, bucket_table, tokens, norm_gain, *, dp, tp):
    _, height, _ = master.shape
    share = tokens.shape[1]
    features = norm_gain.shape[0]
    count = bucket_table.shape[1]
    parts = tp
    members = dp // parts
    assert count // 2 == parts and share * tp == features and height * dp == features
    mine = lax.axis_index("dp")
    column = lax.axis_index("tensor")
    row = mine // members
    place = jnp.stack([row, column, mine % members]).astype(jnp.int32)
    table = bucket_table

    def swap_dp(value, bits):
        return lax.ppermute(value, "dp", [(i, i ^ bits) for i in range(dp)])

    def swap_tensor(value, bits):
        return lax.ppermute(value, "tensor", [(i, i ^ bits) for i in range(tp)])

    half = tokens.shape[0] // 2
    flips = (0, tp // 2)
    near = lax.slice_in_dim(tokens, 0, half, axis=0)
    far = swap_tensor(lax.slice_in_dim(tokens, half, 2 * half, axis=0), tp // 2)

    def turn(value, flip):
        pairs = []
        for q in range(parts):
            for r in range(members):
                for j in range(tp):
                    target = ((j ^ flip) * members + r) * tp + (q ^ flip)
                    pairs.append(((q * members + r) * tp + j, target))
        return lax.ppermute(value, ("dp", "tensor"), pairs)

    new_momentum, update, *grams = local_grams(table, place, momentum, gradient, parts)

    local_f = tokens.astype(f32)
    sums = jnp.sum(local_f * local_f, axis=1)
    bits = tp // 2
    while bits:
        sums = sums + swap_tensor(sums, bits)
        bits //= 2

    sent = [turn(after(value, grams[0]), flip) for value, flip in zip((near, far), flips)]
    total = grams[0]
    for k in range(1, parts):
        total = total + swap_dp(grams[k], k * members)
    pieces = [total]
    bits = 1
    while bits < members:
        pieces = [sum(pieces), swap_dp(sum(pieces), bits)]
        bits *= 2
    step_scale = learn_rate * math.sqrt(max(1.0, features / (2.0 * HD)))
    own = series(pieces, sums.reshape(-1, HD), step_scale)

    packed = [own] + [swap_dp(own, k * members) for k in range(1, parts)]
    lead, factors = lead_weights(table, place, packed, update, master, CHUNKS)
    new_master, *others = apply_update(table, factors, update, master, CHUNKS)

    gain = lax.dynamic_slice_in_dim(norm_gain, row * share, share, 0)[None, :]
    normed = []
    for side in range(2):
        held = {side * (tp // 2): after(sent[side], own)}
        bits = tp // 2
        while bits:
            fresh = {}
            for offset, value in held.items():
                if bits < tp // 2:
                    value = after(value, others[0] if side and others else lead)
                fresh[offset ^ bits] = swap_tensor(value, bits)
            held.update(fresh)
            bits //= 2
        halves = [held[offset] for offset in range(parts)]
        normed.append(normalise(place, halves, packed, gain, side * half, features))

    pieces = []
    for piece in [lead] + others:
        gathered = [piece] + [swap_dp(piece, k) for k in range(1, members)]
        partial = project(place, *normed, gathered)
        sums_of = [swap_dp(partial[k], k * members) for k in range(1, parts)]
        pieces.append([partial[0]] + sums_of)
    return (new_master, new_momentum, finish(pieces))


def solution(mesh):
    placed = (
        P(None, "dp", "tensor"),
        P(None, "dp", "tensor"),
        P(None, "dp", "tensor"),
        P("tensor", None),
        P("dp", "tensor"),
        P(),
    )

    def step(*args):
        return per_device(*args, dp=mesh.shape["dp"], tp=mesh.shape["tensor"])

    return jax.shard_map(
        step,
        mesh=mesh,
        in_specs=placed,
        out_specs=(P(None, "dp", "tensor"), P(None, "dp", "tensor"), P("dp", "tensor")),
        check_vma=False,
    )
```

```python
import functools
import math

import jax
import jax.numpy as jnp
from jax import lax
from jax.experimental import pallas as pl
from jax.experimental.pallas import tpu as pltpu
from jax.sharding import PartitionSpec as P


HD = 128
NS_ITERS = 3

beta_momentum = 0.95
learn_rate = 0.05
first_coeff = 3.4445
cube_coeff = -4.775
fifth_coeff = 2.0315
frob_epsilon = 1e-07
rms_epsilon = 1e-05

CHUNKS = 2
ROWS = 256
MIB = 1 << 20
PLACES = 3
CODE_ROWS = 16
CODE_BITS = 14.9
LEAST = 2.0**-100

bf16 = jnp.bfloat16
f32 = jnp.float32
HIGHEST = lax.Precision.HIGHEST
VM = pl.BlockSpec(memory_space=pltpu.VMEM)
SM = pl.BlockSpec(memory_space=pltpu.SMEM)


def head_of(table, place, count):
    bucket = place // 2
    lower = jnp.int32(0)
    upper = jnp.int32(0)
    for i in range(count):
        j = count - 1 - i
        lower = jnp.where(table[PLACES + j] == bucket, j, lower)
        upper = jnp.where(table[PLACES + i] == bucket, i, upper)
    return jnp.where(place % 2 == 0, lower, upper)


def grid_masks(size):
    rows = lax.broadcasted_iota(jnp.int32, (size, size), 0)
    cols = lax.broadcasted_iota(jnp.int32, (size, size), 1)
    return rows, cols


def pack_symmetric(full):
    half = full.shape[0] // 2
    rows, cols = grid_masks(half)
    low = full[half:, half:]
    mixed = jnp.where(rows <= cols, full[:half, :half], low)
    diag = jnp.sum(jnp.where(rows == cols, low, 0.0), axis=0, keepdims=True)
    return mixed, full[:half, half:], jnp.broadcast_to(diag, (8, half))


def unpack_symmetric(packed):
    half = packed.shape[1]
    mixed = packed[:half]
    side = packed[half : 2 * half]
    diag = packed[2 * half : 2 * half + 1]
    rows, cols = grid_masks(half)
    turned = mixed.T
    first = jnp.where(rows <= cols, mixed, turned)
    low = jnp.where(rows > cols, mixed, jnp.where(rows == cols, diag, turned))
    return jnp.concatenate(
        [
            jnp.concatenate([first, side], axis=1),
            jnp.concatenate([side.T, low], axis=1),
        ],
        axis=0,
    )


def store_packed(ref, full):
    half = full.shape[0] // 2
    mixed, side, diag = pack_symmetric(full)
    ref[0:half, :] = mixed
    ref[half : 2 * half, :] = side
    ref[2 * half : 2 * half + 8, :] = diag


def dot_t(a, b):
    return lax.dot_general(a, b, (((0,), (0,)), ((), ())), preferred_element_type=f32)


def dot_full(a, b):
    return lax.dot_general(
        a, b, (((1,), (0,)), ((), ())), precision=HIGHEST, preferred_element_type=f32
    )


def bucket_side(table, head):
    side = jnp.int32(0)
    for i in range(head):
        side = jnp.where(table[PLACES + i] == table[PLACES + head], 1, side)
    return side


def gram_kernel(place, momentum, gradient, new_momentum, update, *rest, parts):
    outs = rest[:parts]
    held, slopes, split, total, arrive, leave = rest[parts:]
    layers, height, width = update.shape
    slots = width // HD
    tall = split.shape[1]
    wide = 2 * HD
    blocks = [slice(low, low + tall) for low in range(0, height, tall)]
    loads = []
    for i, rows in enumerate(blocks):
        loads.append(
            (
                pltpu.make_async_copy(momentum.at[:, rows, :], held.at[:, rows, :], arrive.at[0, i]),
                pltpu.make_async_copy(gradient.at[:, rows, :], slopes.at[:, rows, :], arrive.at[1, i]),
            )
        )
        for load in loads[-1]:
            load.start()
    stores = []
    for i, rows in enumerate(blocks):
        for load in loads[i]:
            load.wait()
        for head in range(layers * slots):
            layer = head // slots
            cols = slice((head % slots) * HD, (head % slots + 1) * HD)
            slope = slopes[layer, rows, cols]
            fresh = beta_momentum * held[layer, rows, cols] + slope
            held[layer, rows, cols] = fresh
            change = slope + beta_momentum * fresh
            update[layer, rows, cols] = change
            side = bucket_side(place, head)
            for k, plane in enumerate(split_three(change)):
                start = pl.multiple_of(k * wide + side * HD, HD)
                split[place[PLACES + head], :, pl.ds(start, HD)] = plane
        stores.append(
            pltpu.make_async_copy(held.at[:, rows, :], new_momentum.at[:, rows, :], leave.at[i])
        )
        stores[-1].start()
        for bucket in range(parts):
            planes = split[bucket]
            two = planes[:, wide : 2 * wide]
            mixed = dot_t(planes[:, :wide], planes)
            rough = mixed[:, :wide] + dot_t(two, two)
            rough = rough + 2.0 * (mixed[:, wide : 2 * wide] + mixed[:, 2 * wide :])
            if i > 0:
                rough = total[bucket] + rough
            if i + 1 < len(blocks):
                total[bucket] = rough
                continue
            mixed, side, diag = pack_symmetric(0.5 * (rough + rough.T))
            away = bucket ^ place[0]
            for k in range(parts):

                @pl.when(away == k)
                def _():
                    outs[k][0:HD, :] = mixed
                    outs[k][HD : 2 * HD, :] = side
                    outs[k][2 * HD : 2 * HD + 8, :] = diag

    for store in stores:
        store.wait()


def local_grams(place, momentum, gradient, parts):
    shape = momentum.shape
    tall = min(shape[1], ROWS)
    blocks = shape[1] // tall
    packed = (2 * HD + 8, HD)
    anywhere = pl.BlockSpec(memory_space=pl.ANY)
    return pl.pallas_call(
        functools.partial(gram_kernel, parts=parts),
        in_specs=[SM, anywhere, anywhere],
        out_specs=[anywhere] + [VM] * (parts + 1),
        scratch_shapes=[
            pltpu.VMEM(shape, f32),
            pltpu.VMEM(shape, f32),
            pltpu.VMEM((parts, tall, 6 * HD), bf16),
            pltpu.VMEM((parts, 2 * HD, 2 * HD), f32),
            pltpu.SemaphoreType.DMA((2, blocks)),
            pltpu.SemaphoreType.DMA((blocks,)),
        ],
        out_shape=[jax.ShapeDtypeStruct(shape, f32), pltpu.VMEM(shape, f32)]
        + [pltpu.VMEM(packed, f32)] * parts,
        compiler_params=pltpu.CompilerParams(vmem_limit_bytes=16 * MIB),
        name="grams",
    )(place, hbm(momentum), hbm(gradient))


def series_kernel(*refs, step_scale):
    *pieces, sums, out = refs
    packed = pieces[0][...]
    for ref in pieces[1:]:
        packed = packed + ref[...]
    total = unpack_symmetric(packed)
    rows, cols = grid_masks(total.shape[0])
    on_diag = rows == cols
    trace = jnp.sum(jnp.where(on_diag, total, 0.0), keepdims=True)
    scale = 1.0 / (jnp.sqrt(trace) + frob_epsilon)
    gram = total * (scale * scale)
    product = None
    for iteration in range(NS_ITERS):
        square = dot_full(gram, gram)
        factor = cube_coeff * gram + fifth_coeff * square
        factor = factor + jnp.where(on_diag, first_coeff, 0.0)
        product = factor if product is None else dot_full(product, factor)
        if iteration + 1 < NS_ITERS:
            gram = dot_full(dot_full(gram, factor), factor)
    store_packed(out, product * (scale * step_scale))
    high = pieces[0].shape[0]
    out[high : high + 8, :] = jnp.zeros((8, HD), f32)
    out[high : high + sums.shape[0], :] = sums[...]


def hbm(value):
    return pltpu.with_memory_space_constraint(value, pltpu.HBM)


def vmem(value):
    return pltpu.with_memory_space_constraint(value, pltpu.VMEM)


def series(pieces, sums, step_scale):
    high, wide = pieces[0].shape
    return pl.pallas_call(
        functools.partial(series_kernel, step_scale=step_scale),
        in_specs=[VM] * (len(pieces) + 1),
        out_specs=VM,
        out_shape=pltpu.VMEM((high + 8, wide), f32),
        compiler_params=pltpu.CompilerParams(vmem_limit_bytes=5 * MIB),
        name="series",
    )(*[vmem(p) for p in pieces], vmem(sums))


def split_three(value):
    one = value.astype(bf16)
    left = value - one.astype(f32)
    two = left.astype(bf16)
    return one, two, (left - two.astype(f32)).astype(bf16)


def head_pair(update, rows, spots):
    pair = [update[layer, rows, cols] for layer, cols in spots]
    one, two, three = split_three(jnp.concatenate(pair, axis=1))
    return jnp.concatenate([one, one, one, two, two, three], axis=1)


def head_spots(table, bucket, slots, count):
    spots = []
    for side in range(2):
        head = head_of(table, 2 * bucket + side, count)
        spots.append((head // slots, pl.ds(pl.multiple_of(head % slots * HD, HD), HD)))
    return spots


def lead_kernel(place, *refs, parts, slots, heads):
    packed = refs[:parts]
    update, master, weights, factors = refs[parts:]
    layers, height, _ = master.shape
    wide = 2 * HD
    for k in range(parts):
        planes = split_three(unpack_symmetric(packed[k][0 : 2 * HD + 8, :]))
        away = k ^ place[0]
        for spot, plane in enumerate((0, 1, 2, 0, 1, 0)):
            factors[away, spot * wide : (spot + 1) * wide, :] = planes[plane]

    tall = min(height, ROWS)
    for head in range(heads):
        bucket = place[PLACES + head]
        start = pl.multiple_of(bucket_side(place, head) * HD, HD)
        factor = factors[bucket, :, pl.ds(start, HD)]
        spots = head_spots(place, bucket, slots, layers * slots)
        cols = slice(head * HD, (head + 1) * HD)
        for low in range(0, height, tall):
            rows = slice(low, low + tall)
            value = head_pair(update, rows, spots)
            ortho = jnp.dot(value, factor, preferred_element_type=f32)
            weights[rows, cols] = (master[0, rows, cols] - ortho).astype(bf16)


def lead_weights(place, packed, update, master, chunks):
    _, height, width = master.shape
    parts = len(packed)
    slots = width // HD
    return pl.pallas_call(
        functools.partial(lead_kernel, parts=parts, slots=slots, heads=slots // chunks),
        in_specs=[SM] + [VM] * (parts + 2),
        out_specs=[VM, VM],
        out_shape=[
            pltpu.VMEM((height, width // chunks), bf16),
            pltpu.VMEM((parts, 12 * HD, 2 * HD), bf16),
        ],
        compiler_params=pltpu.CompilerParams(vmem_limit_bytes=9 * MIB),
        name="lead",
    )(place, *[vmem(p) for p in packed], vmem(update), vmem(master))


def apply_kernel(table, factors, update, master, new_master, *refs, chunks):
    weights = refs[: chunks - 1]
    fresh, sems = refs[chunks - 1 :]
    layers, height, width = master.shape
    slots = width // HD
    tall = min(height, ROWS)
    piece = width // chunks
    parts = factors.shape[0]
    spots = [head_spots(table, bucket, slots, layers * slots) for bucket in range(parts)]
    copies = []
    for i in range(height // tall):
        rows = slice(i * tall, (i + 1) * tall)
        for bucket in range(parts):
            value = head_pair(update, rows, spots[bucket])
            ortho = jnp.dot(value, factors[bucket], preferred_element_type=f32)
            for side, (layer, cols) in enumerate(spots[bucket]):
                part = ortho[:, side * HD : (side + 1) * HD]
                fresh[layer, rows, cols] = master[layer, rows, cols] - part
        copies.append(
            pltpu.make_async_copy(fresh.at[:, rows, :], new_master.at[:, rows, :], sems.at[i])
        )
        copies[-1].start()
        for c in range(1, chunks):
            cols = slice(c * piece, (c + 1) * piece)
            weights[c - 1][rows, :] = fresh[0, rows, cols].astype(bf16)
    for copy in copies:
        copy.wait()


def apply_update(table, factors, update, master, chunks):
    _, height, width = master.shape
    return pl.pallas_call(
        functools.partial(apply_kernel, chunks=chunks),
        in_specs=[SM] + [VM] * 3,
        out_specs=[pl.BlockSpec(memory_space=pl.ANY)] + [VM] * (chunks - 1),
        scratch_shapes=[
            pltpu.VMEM(master.shape, f32),
            pltpu.SemaphoreType.DMA((height // min(height, ROWS),)),
        ],
        out_shape=[jax.ShapeDtypeStruct(master.shape, f32)]
        + [pltpu.VMEM((height, width // chunks), bf16)] * (chunks - 1),
        compiler_params=pltpu.CompilerParams(vmem_limit_bytes=9 * MIB),
        name="apply",
    )(table, vmem(factors), vmem(update), vmem(master))


def norm_kernel(place, *refs, parts, base, features):
    pieces = refs[:parts]
    packed = refs[parts : 2 * parts]
    gain, out, sums = refs[2 * parts :]
    height, width = pieces[0].shape
    high = packed[0].shape[0] - 8
    for k in range(parts):
        sums[k] = lax.rsqrt(packed[k][high : high + 8, :] / features + rms_epsilon)
    for k in range(parts):
        away = k ^ place[0] ^ place[1]
        inverse = sums[away]
        for low in range(0, height, HD):
            spot = (base + low) // HD
            column = jnp.broadcast_to(inverse[spot : spot + 1, :], (HD, HD)).T
            for left in range(0, width, HD):
                cols = slice(left, left + HD)
                values = pieces[k][low : low + HD, cols].astype(f32)
                out[away, low : low + HD, cols] = (values * column * gain[:, cols]).astype(bf16)


def normalise(place, pieces, packed, gain, base, features):
    parts = len(packed)
    height, width = pieces[0].shape
    return pl.pallas_call(
        functools.partial(norm_kernel, parts=parts, base=base, features=features),
        in_specs=[SM] + [VM] * (2 * parts + 1),
        out_specs=VM,
        out_shape=pltpu.VMEM((parts, height, width), bf16),
        scratch_shapes=[pltpu.VMEM((parts, 8, HD), f32)],
        compiler_params=pltpu.CompilerParams(vmem_limit_bytes=5 * MIB),
        name="normalise",
    )(place, *[vmem(p) for p in pieces], *[vmem(p) for p in packed], vmem(gain))


def project_kernel(place, near, far, *refs, members, parts):
    weights = refs[:members]
    outs = refs[members : members + parts]
    whole = refs[-1]
    height = weights[0].shape[0]
    for k in range(members):
        start = pl.multiple_of((k ^ place[2]) * height, height)
        whole[pl.ds(start, height), :] = weights[k][...]
    for m in range(parts):
        both = jnp.concatenate([near[m], far[m]], axis=0)
        part = jnp.dot(both, whole[...], preferred_element_type=f32)
        if m == 0:
            outs[m][...] = part
        else:
            encode(outs[m], part)


def encode(out, value):
    height = value.shape[0]
    top = jnp.max(jnp.abs(value), axis=0, keepdims=True)
    power = jnp.ceil(jnp.log2(jnp.maximum(top, LEAST)) - CODE_BITS)
    code = jnp.round(value * jnp.exp2(-power))
    out[0:height, :] = code.astype(jnp.int32).astype(jnp.int16)
    tail = jnp.broadcast_to(power, (CODE_ROWS, value.shape[1]))
    out[height : height + CODE_ROWS, :] = tail.astype(jnp.int32).astype(jnp.int16)


def finish_kernel(*refs, chunks, parts):
    out = refs[-1]
    for c in range(chunks):
        own, *codes = refs[c * parts : (c + 1) * parts]
        height, width = own.shape
        total = own[...]
        for code in codes:
            power = code[height : height + CODE_ROWS, :].astype(jnp.int32).astype(f32)
            value = code[0:height, :].astype(jnp.int32).astype(f32)
            total = total + value * jnp.exp2(power[0:1, :])
        out[:, c * width : (c + 1) * width] = total.astype(bf16)


def finish(pieces):
    chunks = len(pieces)
    parts = len(pieces[0])
    height, width = pieces[0][0].shape
    return pl.pallas_call(
        functools.partial(finish_kernel, chunks=chunks, parts=parts),
        in_specs=[VM] * (chunks * parts),
        out_shape=jax.ShapeDtypeStruct((height, chunks * width), bf16),
        compiler_params=pltpu.CompilerParams(vmem_limit_bytes=5 * MIB),
        name="finish",
    )(*[vmem(p) for piece in pieces for p in piece])


def project(place, near, far, weights):
    parts, height, width = near.shape
    height *= 2
    cols = weights[0].shape[1]
    code = pltpu.VMEM((height + CODE_ROWS, cols), jnp.int16)
    return pl.pallas_call(
        functools.partial(project_kernel, members=len(weights), parts=parts),
        in_specs=[SM] + [VM] * (2 + len(weights)),
        out_specs=[VM] * parts,
        out_shape=[pltpu.VMEM((height, cols), f32)] + [code] * (parts - 1),
        scratch_shapes=[pltpu.VMEM((width, cols), bf16)],
        compiler_params=pltpu.CompilerParams(vmem_limit_bytes=5 * MIB),
        name="project",
    )(place, vmem(near), vmem(far), *[vmem(w) for w in weights])


def after(value, other):
    return lax.optimization_barrier((value, other))[0]


def per_device(master, momentum, gradient, bucket_table, tokens, norm_gain, *, dp, tp):
    _, height, _ = master.shape
    share = tokens.shape[1]
    features = norm_gain.shape[0]
    count = bucket_table.shape[1]
    parts = tp
    members = dp // parts
    assert count // 2 == parts and share * tp == features and height * dp == features
    mine = lax.axis_index("dp")
    column = lax.axis_index("tensor")
    row = mine // members
    spot = jnp.stack([row, column, mine % members]).astype(jnp.int32)
    place = jnp.concatenate([spot, bucket_table[0]])

    def swap_dp(value, bits):
        return lax.ppermute(value, "dp", [(i, i ^ bits) for i in range(dp)])

    def swap_tensor(value, bits):
        return lax.ppermute(value, "tensor", [(i, i ^ bits) for i in range(tp)])

    half = tokens.shape[0] // 2
    flips = (0, tp // 2)
    far = swap_tensor(lax.slice_in_dim(tokens, half, 2 * half, axis=0), tp // 2)

    def turn(value, flip):
        pairs = []
        for q in range(parts):
            for r in range(members):
                for j in range(tp):
                    target = ((j ^ flip) * members + r) * tp + (q ^ flip)
                    pairs.append(((q * members + r) * tp + j, target))
        return lax.ppermute(value, ("dp", "tensor"), pairs)

    new_momentum, update, *grams = local_grams(place, momentum, gradient, parts)

    local_f = tokens.astype(f32)
    sums = jnp.sum(local_f * local_f, axis=1)
    bits = tp // 2
    while bits:
        sums = sums + swap_tensor(sums, bits)
        bits //= 2

    near = lax.slice_in_dim(after(tokens, grams[0]), 0, half, axis=0)
    sent = [turn(near, flips[0]), turn(after(far, grams[0]), flips[1])]
    total = grams[0]
    for k in range(1, parts):
        total = total + swap_dp(grams[k], k * members)
    pieces = [total]
    bits = 1
    while bits < members:
        pieces = [sum(pieces), swap_dp(sum(pieces), bits)]
        bits *= 2
    step_scale = learn_rate * math.sqrt(max(1.0, features / (2.0 * HD)))
    own = series(pieces, sums.reshape(-1, HD), step_scale)

    packed = [own] + [swap_dp(own, k * members) for k in range(1, parts)]
    lead, factors = lead_weights(place, packed, update, master, CHUNKS)
    gain = lax.dynamic_slice_in_dim(norm_gain, row * share, share, 0)[None, :]

    def shared(side, start):
        held = {side * (tp // 2): after(sent[side], own)}
        bits = tp // 2
        while bits:
            fresh = {}
            for offset, value in held.items():
                if bits < tp // 2:
                    value = after(value, start)
                fresh[offset ^ bits] = swap_tensor(value, bits)
            held.update(fresh)
            bits //= 2
        halves = [held[offset] for offset in range(parts)]
        return normalise(place, halves, packed, gain, side * half, features)

    near_normed = shared(0, lead)
    new_master, *others = apply_update(place, factors, update, master, CHUNKS)
    normed = (near_normed, shared(1, others[0] if others else lead))

    pieces = []
    for piece in [lead] + others:
        gathered = [piece] + [swap_dp(piece, k) for k in range(1, members)]
        partial = project(place, *normed, gathered)
        sums_of = [swap_dp(partial[k], k * members) for k in range(1, parts)]
        pieces.append([partial[0]] + sums_of)
    return (new_master, new_momentum, finish(pieces))


def solution(mesh):
    placed = (
        P(None, "dp", "tensor"),
        P(None, "dp", "tensor"),
        P(None, "dp", "tensor"),
        P("tensor", None),
        P("dp", "tensor"),
        P(),
    )

    def step(*args):
        return per_device(*args, dp=mesh.shape["dp"], tp=mesh.shape["tensor"])

    return jax.shard_map(
        step,
        mesh=mesh,
        in_specs=placed,
        out_specs=(P(None, "dp", "tensor"), P(None, "dp", "tensor"), P("dp", "tensor")),
        check_vma=False,
    )
```

```python
import functools
import math

import jax
import jax.numpy as jnp
from jax import lax
from jax.experimental import pallas as pl
from jax.experimental.pallas import tpu as pltpu
from jax.sharding import PartitionSpec as P


HD = 128
NS_ITERS = 3

beta_momentum = 0.95
learn_rate = 0.05
first_coeff = 3.4445
cube_coeff = -4.775
fifth_coeff = 2.0315
frob_epsilon = 1e-07
rms_epsilon = 1e-05

CHUNKS = 2
ROWS = 256
MIB = 1 << 20
PLACES = 3
CODE_ROWS = 8
CODE_BITS = 14.9
LEAST = 2.0**-100

bf16 = jnp.bfloat16
f32 = jnp.float32
HIGHEST = lax.Precision.HIGHEST
VM = pl.BlockSpec(memory_space=pltpu.VMEM)
SM = pl.BlockSpec(memory_space=pltpu.SMEM)


def head_of(table, place, count):
    bucket = place // 2
    lower = jnp.int32(0)
    upper = jnp.int32(0)
    for i in range(count):
        j = count - 1 - i
        lower = jnp.where(table[PLACES + j] == bucket, j, lower)
        upper = jnp.where(table[PLACES + i] == bucket, i, upper)
    return jnp.where(place % 2 == 0, lower, upper)


def grid_masks(size):
    rows = lax.broadcasted_iota(jnp.int32, (size, size), 0)
    cols = lax.broadcasted_iota(jnp.int32, (size, size), 1)
    return rows, cols


def pack_symmetric(full):
    half = full.shape[0] // 2
    rows, cols = grid_masks(half)
    low = full[half:, half:]
    mixed = jnp.where(rows <= cols, full[:half, :half], low)
    diag = jnp.sum(jnp.where(rows == cols, low, 0.0), axis=0, keepdims=True)
    return mixed, full[:half, half:], jnp.broadcast_to(diag, (8, half))


def unpack_symmetric(packed):
    half = packed.shape[1]
    mixed = packed[:half]
    side = packed[half : 2 * half]
    diag = packed[2 * half : 2 * half + 1]
    rows, cols = grid_masks(half)
    turned = mixed.T
    first = jnp.where(rows <= cols, mixed, turned)
    low = jnp.where(rows > cols, mixed, jnp.where(rows == cols, diag, turned))
    return jnp.concatenate(
        [
            jnp.concatenate([first, side], axis=1),
            jnp.concatenate([side.T, low], axis=1),
        ],
        axis=0,
    )


def store_packed(ref, full):
    half = full.shape[0] // 2
    mixed, side, diag = pack_symmetric(full)
    ref[0:half, :] = mixed
    ref[half : 2 * half, :] = side
    ref[2 * half : 2 * half + 8, :] = diag


def dot_t(a, b):
    return lax.dot_general(a, b, (((0,), (0,)), ((), ())), preferred_element_type=f32)


def dot_full(a, b):
    return lax.dot_general(
        a, b, (((1,), (0,)), ((), ())), precision=HIGHEST, preferred_element_type=f32
    )


def bucket_side(table, head):
    side = jnp.int32(0)
    for i in range(head):
        side = jnp.where(table[PLACES + i] == table[PLACES + head], 1, side)
    return side


def gram_kernel(place, momentum, gradient, new_momentum, update, *rest, parts):
    outs = rest[:parts]
    held, slopes, split, total, arrive, leave = rest[parts:]
    layers, height, width = update.shape
    slots = width // HD
    tall = split.shape[1]
    wide = 2 * HD
    blocks = [slice(low, low + tall) for low in range(0, height, tall)]
    loads = []
    for i, rows in enumerate(blocks):
        loads.append(
            (
                pltpu.make_async_copy(momentum.at[:, rows, :], held.at[:, rows, :], arrive.at[0, i]),
                pltpu.make_async_copy(gradient.at[:, rows, :], slopes.at[:, rows, :], arrive.at[1, i]),
            )
        )
        for load in loads[-1]:
            load.start()
    stores = []
    for i, rows in enumerate(blocks):
        for load in loads[i]:
            load.wait()
        for head in range(layers * slots):
            layer = head // slots
            cols = slice((head % slots) * HD, (head % slots + 1) * HD)
            slope = slopes[layer, rows, cols]
            fresh = beta_momentum * held[layer, rows, cols] + slope
            held[layer, rows, cols] = fresh
            change = slope + beta_momentum * fresh
            update[layer, rows, cols] = change
            side = bucket_side(place, head)
            for k, plane in enumerate(split_three(change)):
                start = pl.multiple_of(k * wide + side * HD, HD)
                split[place[PLACES + head], :, pl.ds(start, HD)] = plane
        stores.append(
            pltpu.make_async_copy(held.at[:, rows, :], new_momentum.at[:, rows, :], leave.at[i])
        )
        stores[-1].start()
        for bucket in range(parts):
            planes = split[bucket]
            two = planes[:, wide : 2 * wide]
            mixed = dot_t(planes[:, :wide], planes)
            rough = mixed[:, :wide] + dot_t(two, two)
            rough = rough + 2.0 * (mixed[:, wide : 2 * wide] + mixed[:, 2 * wide :])
            if i > 0:
                rough = total[bucket] + rough
            if i + 1 < len(blocks):
                total[bucket] = rough
                continue
            mixed, side, diag = pack_symmetric(0.5 * (rough + rough.T))
            away = bucket ^ place[0]
            for k in range(parts):

                @pl.when(away == k)
                def _():
                    outs[k][0:HD, :] = mixed
                    outs[k][HD : 2 * HD, :] = side
                    outs[k][2 * HD : 2 * HD + 8, :] = diag

    for store in stores:
        store.wait()


def local_grams(place, momentum, gradient, parts):
    shape = momentum.shape
    tall = min(shape[1], ROWS)
    blocks = shape[1] // tall
    packed = (2 * HD + 8, HD)
    anywhere = pl.BlockSpec(memory_space=pl.ANY)
    return pl.pallas_call(
        functools.partial(gram_kernel, parts=parts),
        in_specs=[SM, anywhere, anywhere],
        out_specs=[anywhere] + [VM] * (parts + 1),
        scratch_shapes=[
            pltpu.VMEM(shape, f32),
            pltpu.VMEM(shape, f32),
            pltpu.VMEM((parts, tall, 6 * HD), bf16),
            pltpu.VMEM((parts, 2 * HD, 2 * HD), f32),
            pltpu.SemaphoreType.DMA((2, blocks)),
            pltpu.SemaphoreType.DMA((blocks,)),
        ],
        out_shape=[jax.ShapeDtypeStruct(shape, f32), pltpu.VMEM(shape, f32)]
        + [pltpu.VMEM(packed, f32)] * parts,
        compiler_params=pltpu.CompilerParams(vmem_limit_bytes=16 * MIB),
        name="grams",
    )(place, hbm(momentum), hbm(gradient))


def series_kernel(*refs, step_scale):
    *pieces, sums, out = refs
    packed = pieces[0][...]
    for ref in pieces[1:]:
        packed = packed + ref[...]
    total = unpack_symmetric(packed)
    rows, cols = grid_masks(total.shape[0])
    on_diag = rows == cols
    trace = jnp.sum(jnp.where(on_diag, total, 0.0), keepdims=True)
    scale = 1.0 / (jnp.sqrt(trace) + frob_epsilon)
    gram = total * (scale * scale)
    product = None
    for iteration in range(NS_ITERS):
        square = dot_full(gram, gram)
        factor = cube_coeff * gram + fifth_coeff * square
        factor = factor + jnp.where(on_diag, first_coeff, 0.0)
        product = factor if product is None else dot_full(product, factor)
        if iteration + 1 < NS_ITERS:
            gram = dot_full(dot_full(gram, factor), factor)
    store_packed(out, product * (scale * step_scale))
    first = pieces[0].shape[0] - 7
    out[first : first + sums.shape[0], :] = sums[...]


def hbm(value):
    return pltpu.with_memory_space_constraint(value, pltpu.HBM)


def vmem(value):
    return pltpu.with_memory_space_constraint(value, pltpu.VMEM)


def series(pieces, sums, step_scale):
    high, wide = pieces[0].shape
    return pl.pallas_call(
        functools.partial(series_kernel, step_scale=step_scale),
        in_specs=[VM] * (len(pieces) + 1),
        out_specs=VM,
        out_shape=pltpu.VMEM((high, wide), f32),
        compiler_params=pltpu.CompilerParams(vmem_limit_bytes=5 * MIB),
        name="series",
    )(*[vmem(p) for p in pieces], vmem(sums))


def split_three(value):
    one = value.astype(bf16)
    left = value - one.astype(f32)
    two = left.astype(bf16)
    return one, two, (left - two.astype(f32)).astype(bf16)


def head_pair(update, rows, spots):
    pair = [update[layer, rows, cols] for layer, cols in spots]
    one, two, three = split_three(jnp.concatenate(pair, axis=1))
    return jnp.concatenate([one, one, one, two, two, three], axis=1)


def head_spots(table, bucket, slots, count):
    spots = []
    for side in range(2):
        head = head_of(table, 2 * bucket + side, count)
        spots.append((head // slots, pl.ds(pl.multiple_of(head % slots * HD, HD), HD)))
    return spots


def lead_kernel(place, *refs, parts, slots, heads):
    packed = refs[:parts]
    update, master, weights, factors = refs[parts:]
    wide = 2 * HD
    for k in range(parts):
        planes = split_three(unpack_symmetric(packed[k][0 : 2 * HD + 8, :]))
        away = k ^ place[0]
        for spot, plane in enumerate((0, 1, 2, 0, 1, 0)):
            factors[away, spot * wide : (spot + 1) * wide, :] = planes[plane]

    store_weights(place, factors, update, master, weights, slots, range(heads))


def store_weights(place, factors, update, master, weights, slots, heads):
    layers, height, _ = master.shape
    tall = min(height, ROWS)
    for spot, head in enumerate(heads):
        bucket = place[PLACES + head]
        start = pl.multiple_of(bucket_side(place, head) * HD, HD)
        factor = factors[bucket, :, pl.ds(start, HD)]
        spots = head_spots(place, bucket, slots, layers * slots)
        cols = slice(head * HD, (head + 1) * HD)
        for low in range(0, height, tall):
            rows = slice(low, low + tall)
            value = head_pair(update, rows, spots)
            ortho = jnp.dot(value, factor, preferred_element_type=f32)
            rounded = (master[0, rows, cols] - ortho).astype(bf16)
            weights[rows, spot * HD : (spot + 1) * HD] = rounded


def lead_weights(place, packed, update, master, chunks):
    _, height, width = master.shape
    parts = len(packed)
    slots = width // HD
    return pl.pallas_call(
        functools.partial(lead_kernel, parts=parts, slots=slots, heads=slots // chunks),
        in_specs=[SM] + [VM] * (parts + 2),
        out_specs=[VM, VM],
        out_shape=[
            pltpu.VMEM((height, width // chunks), bf16),
            pltpu.VMEM((parts, 12 * HD, 2 * HD), bf16),
        ],
        compiler_params=pltpu.CompilerParams(vmem_limit_bytes=9 * MIB),
        name="lead",
    )(place, *[vmem(p) for p in packed], vmem(update), vmem(master))


def next_kernel(place, factors, update, master, weights, *, slots, heads):
    store_weights(place, factors, update, master, weights, slots, heads)


def next_weights(place, factors, update, master, chunks, chunk):
    _, height, width = master.shape
    slots = width // HD
    share = slots // chunks
    heads = range(chunk * share, (chunk + 1) * share)
    return pl.pallas_call(
        functools.partial(next_kernel, slots=slots, heads=heads),
        in_specs=[SM] + [VM] * 3,
        out_specs=VM,
        out_shape=pltpu.VMEM((height, width // chunks), bf16),
        compiler_params=pltpu.CompilerParams(vmem_limit_bytes=9 * MIB),
        name="next",
    )(place, vmem(factors), vmem(update), vmem(master))


def apply_kernel(place, factors, update, master, new_master, changes, fresh, arrive, leave):
    layers, height, width = master.shape
    slots = width // HD
    tall = min(height, ROWS)
    parts = factors.shape[0]
    blocks = [slice(low, low + tall) for low in range(0, height, tall)]
    loads = []
    for i, rows in enumerate(blocks):
        loads.append(
            (
                pltpu.make_async_copy(update.at[:, rows, :], changes.at[:, rows, :], arrive.at[0, i]),
                pltpu.make_async_copy(master.at[:, rows, :], fresh.at[:, rows, :], arrive.at[1, i]),
            )
        )
        for load in loads[-1]:
            load.start()
    spots = [head_spots(place, bucket, slots, layers * slots) for bucket in range(parts)]
    stores = []
    for i, rows in enumerate(blocks):
        for load in loads[i]:
            load.wait()
        for bucket in range(parts):
            value = head_pair(changes, rows, spots[bucket])
            ortho = jnp.dot(value, factors[bucket], preferred_element_type=f32)
            for side, (layer, cols) in enumerate(spots[bucket]):
                part = ortho[:, side * HD : (side + 1) * HD]
                fresh[layer, rows, cols] = fresh[layer, rows, cols] - part
        stores.append(
            pltpu.make_async_copy(fresh.at[:, rows, :], new_master.at[:, rows, :], leave.at[i])
        )
        stores[-1].start()
    for store in stores:
        store.wait()


def apply_update(place, factors, update, master):
    blocks = master.shape[1] // min(master.shape[1], ROWS)
    anywhere = pl.BlockSpec(memory_space=pl.ANY)
    return pl.pallas_call(
        apply_kernel,
        in_specs=[SM, VM, anywhere, anywhere],
        out_specs=anywhere,
        scratch_shapes=[
            pltpu.VMEM(master.shape, f32),
            pltpu.VMEM(master.shape, f32),
            pltpu.SemaphoreType.DMA((2, blocks)),
            pltpu.SemaphoreType.DMA((blocks,)),
        ],
        out_shape=jax.ShapeDtypeStruct(master.shape, f32),
        compiler_params=pltpu.CompilerParams(vmem_limit_bytes=13 * MIB),
        name="apply",
    )(place, vmem(factors), hbm(update), hbm(master))


def norm_kernel(place, *refs, parts, base, features):
    pieces = refs[:parts]
    packed = refs[parts : 2 * parts]
    gain, out, sums = refs[2 * parts :]
    height, width = pieces[0].shape
    high = packed[0].shape[0] - 8
    for k in range(parts):
        sums[k] = lax.rsqrt(packed[k][high : high + 8, :] / features + rms_epsilon)
    for k in range(parts):
        away = k ^ place[0] ^ place[1]
        inverse = sums[away]
        for low in range(0, height, HD):
            spot = 1 + (base + low) // HD
            column = jnp.broadcast_to(inverse[spot : spot + 1, :], (HD, HD)).T
            for left in range(0, width, HD):
                cols = slice(left, left + HD)
                own = pl.ds(pl.multiple_of(place[0] * width + left, HD), HD)
                values = pieces[k][low : low + HD, cols].astype(f32)
                out[away, low : low + HD, cols] = (values * column * gain[:, own]).astype(bf16)


def normalise(place, pieces, packed, gain, base, features):
    parts = len(packed)
    height, width = pieces[0].shape
    return pl.pallas_call(
        functools.partial(norm_kernel, parts=parts, base=base, features=features),
        in_specs=[SM] + [VM] * (2 * parts + 1),
        out_specs=VM,
        out_shape=pltpu.VMEM((parts, height, width), bf16),
        scratch_shapes=[pltpu.VMEM((parts, 8, HD), f32)],
        compiler_params=pltpu.CompilerParams(vmem_limit_bytes=5 * MIB),
        name="normalise",
    )(place, *[vmem(p) for p in pieces], *[vmem(p) for p in packed], vmem(gain))


def project_kernel(place, near, far, *refs, members, parts):
    weights = refs[:members]
    outs = refs[members : members + parts]
    whole = refs[-1]
    height = weights[0].shape[0]
    for k in range(members):
        start = pl.multiple_of((k ^ place[2]) * height, height)
        whole[pl.ds(start, height), :] = weights[k][...]
    for m in range(parts):
        both = jnp.concatenate([near[m], far[m]], axis=0)
        part = jnp.dot(both, whole[...], preferred_element_type=f32)
        if m == 0:
            outs[m][...] = part
        else:
            encode(outs[m], part)


def encode(out, value):
    height = value.shape[0]
    top = jnp.max(jnp.abs(value), axis=0, keepdims=True)
    power = jnp.ceil(jnp.log2(jnp.maximum(top, LEAST)) - CODE_BITS)
    code = jnp.round(value * jnp.exp2(-power))
    out[0:height, :] = code.astype(jnp.int32).astype(jnp.int16)
    tail = jnp.broadcast_to(power, (CODE_ROWS, value.shape[1]))
    out[height : height + CODE_ROWS, :] = tail.astype(jnp.int32).astype(jnp.int16)


def finish_kernel(*refs, chunks, parts):
    out = refs[-1]
    for c in range(chunks):
        own, *codes = refs[c * parts : (c + 1) * parts]
        height, width = own.shape
        total = own[...]
        for code in codes:
            power = code[height : height + CODE_ROWS, :].astype(jnp.int32).astype(f32)
            value = code[0:height, :].astype(jnp.int32).astype(f32)
            total = total + value * jnp.exp2(power[0:1, :])
        out[:, c * width : (c + 1) * width] = total.astype(bf16)


def finish(pieces):
    chunks = len(pieces)
    parts = len(pieces[0])
    height, width = pieces[0][0].shape
    return pl.pallas_call(
        functools.partial(finish_kernel, chunks=chunks, parts=parts),
        in_specs=[VM] * (chunks * parts),
        out_shape=jax.ShapeDtypeStruct((height, chunks * width), bf16),
        compiler_params=pltpu.CompilerParams(vmem_limit_bytes=5 * MIB),
        name="finish",
    )(*[vmem(p) for piece in pieces for p in piece])


def project(place, near, far, weights):
    parts, height, width = near.shape
    height *= 2
    cols = weights[0].shape[1]
    code = pltpu.VMEM((height + CODE_ROWS, cols), jnp.int16)
    return pl.pallas_call(
        functools.partial(project_kernel, members=len(weights), parts=parts),
        in_specs=[SM] + [VM] * (2 + len(weights)),
        out_specs=[VM] * parts,
        out_shape=[pltpu.VMEM((height, cols), f32)] + [code] * (parts - 1),
        scratch_shapes=[pltpu.VMEM((width, cols), bf16)],
        compiler_params=pltpu.CompilerParams(vmem_limit_bytes=5 * MIB),
        name="project",
    )(place, vmem(near), vmem(far), *[vmem(w) for w in weights])


def after(value, other):
    return lax.optimization_barrier((value, other))[0]


def per_device(master, momentum, gradient, bucket_table, tokens, norm_gain, *, dp, tp):
    _, height, _ = master.shape
    share = tokens.shape[1]
    features = norm_gain.shape[0]
    count = bucket_table.shape[1]
    parts = tp
    members = dp // parts
    assert count // 2 == parts and share * tp == features and height * dp == features
    mine = lax.axis_index("dp")
    column = lax.axis_index("tensor")
    row = mine // members
    spot = jnp.stack([row, column, mine % members]).astype(jnp.int32)
    place = jnp.concatenate([spot, bucket_table[0]])

    def swap_dp(value, bits):
        return lax.ppermute(value, "dp", [(i, i ^ bits) for i in range(dp)])

    def swap_tensor(value, bits):
        return lax.ppermute(value, "tensor", [(i, i ^ bits) for i in range(tp)])

    half = tokens.shape[0] // 2
    flips = (0, tp // 2)
    far = swap_tensor(lax.slice_in_dim(tokens, half, 2 * half, axis=0), tp // 2)

    def turn(value, flip):
        pairs = []
        for q in range(parts):
            for r in range(members):
                for j in range(tp):
                    target = ((j ^ flip) * members + r) * tp + (q ^ flip)
                    pairs.append(((q * members + r) * tp + j, target))
        return lax.ppermute(value, ("dp", "tensor"), pairs)

    new_momentum, update, *grams = local_grams(place, momentum, gradient, parts)

    local_f = tokens.astype(f32)
    sums = jnp.sum(local_f * local_f, axis=1)
    bits = tp // 2
    while bits:
        sums = sums + swap_tensor(sums, bits)
        bits //= 2

    near = lax.slice_in_dim(after(tokens, grams[0]), 0, half, axis=0)
    sent = [turn(near, flips[0]), turn(after(far, grams[0]), flips[1])]
    total = grams[0]
    for k in range(1, parts):
        total = total + swap_dp(grams[k], k * members)
    pieces = [total]
    bits = 1
    while bits < members:
        pieces = [sum(pieces), swap_dp(sum(pieces), bits)]
        bits *= 2
    step_scale = learn_rate * math.sqrt(max(1.0, features / (2.0 * HD)))
    own = series(pieces, sums.reshape(-1, HD), step_scale)

    packed = [own] + [swap_dp(own, k * members) for k in range(1, parts)]
    lead, factors = lead_weights(place, packed, update, master, CHUNKS)
    gain = norm_gain[None, :]

    def shared(side, start):
        held = {side * (tp // 2): after(sent[side], own)}
        bits = tp // 2
        while bits:
            fresh = {}
            for offset, value in held.items():
                if bits < tp // 2:
                    value = after(value, start)
                fresh[offset ^ bits] = swap_tensor(value, bits)
            held.update(fresh)
            bits //= 2
        halves = [held[offset] for offset in range(parts)]
        return normalise(place, halves, packed, gain, side * half, features)

    others = [next_weights(place, factors, update, master, CHUNKS, c) for c in range(1, CHUNKS)]
    near_normed = shared(0, (others or [lead])[-1])
    normed = (near_normed, shared(1, near_normed))

    pieces = []
    for piece in [lead] + others:
        gathered = [piece] + [swap_dp(piece, k) for k in range(1, members)]
        partial = project(place, *normed, gathered)
        sums_of = [swap_dp(partial[k], k * members) for k in range(1, parts)]
        pieces.append([partial[0]] + sums_of)
    new_master = apply_update(place, factors, update, master)
    return (new_master, new_momentum, finish(pieces))


def solution(mesh):
    placed = (
        P(None, "dp", "tensor"),
        P(None, "dp", "tensor"),
        P(None, "dp", "tensor"),
        P("tensor", None),
        P("dp", "tensor"),
        P(),
    )

    def step(*args):
        return per_device(*args, dp=mesh.shape["dp"], tp=mesh.shape["tensor"])

    return jax.shard_map(
        step,
        mesh=mesh,
        in_specs=placed,
        out_specs=(P(None, "dp", "tensor"), P(None, "dp", "tensor"), P("dp", "tensor")),
        check_vma=False,
    )
```

```python
import functools
import math

import jax
import jax.numpy as jnp
from jax import lax
from jax.experimental import pallas as pl
from jax.experimental.pallas import tpu as pltpu
from jax.sharding import PartitionSpec as P


HD = 128
NS_ITERS = 3

beta_momentum = 0.95
learn_rate = 0.05
first_coeff = 3.4445
cube_coeff = -4.775
fifth_coeff = 2.0315
frob_epsilon = 1e-07
rms_epsilon = 1e-05

CHUNKS = 2
ROWS = 256
MIB = 1 << 20
PLACES = 3
CODE_ROWS = 8
CODE_BITS = 14.9
LEAST = 2.0**-100

bf16 = jnp.bfloat16
f32 = jnp.float32
HIGHEST = lax.Precision.HIGHEST
VM = pl.BlockSpec(memory_space=pltpu.VMEM)
SM = pl.BlockSpec(memory_space=pltpu.SMEM)


def head_of(table, place, count):
    bucket = place // 2
    lower = jnp.int32(0)
    upper = jnp.int32(0)
    for i in range(count):
        j = count - 1 - i
        lower = jnp.where(table[PLACES + j] == bucket, j, lower)
        upper = jnp.where(table[PLACES + i] == bucket, i, upper)
    return jnp.where(place % 2 == 0, lower, upper)


def grid_masks(size):
    rows = lax.broadcasted_iota(jnp.int32, (size, size), 0)
    cols = lax.broadcasted_iota(jnp.int32, (size, size), 1)
    return rows, cols


def pack_symmetric(full):
    half = full.shape[0] // 2
    rows, cols = grid_masks(half)
    low = full[half:, half:]
    mixed = jnp.where(rows <= cols, full[:half, :half], low)
    diag = jnp.sum(jnp.where(rows == cols, low, 0.0), axis=0, keepdims=True)
    return mixed, full[:half, half:], jnp.broadcast_to(diag, (8, half))


def unpack_symmetric(packed):
    half = packed.shape[1]
    mixed = packed[:half]
    side = packed[half : 2 * half]
    diag = packed[2 * half : 2 * half + 1]
    rows, cols = grid_masks(half)
    turned = mixed.T
    first = jnp.where(rows <= cols, mixed, turned)
    low = jnp.where(rows > cols, mixed, jnp.where(rows == cols, diag, turned))
    return jnp.concatenate(
        [
            jnp.concatenate([first, side], axis=1),
            jnp.concatenate([side.T, low], axis=1),
        ],
        axis=0,
    )


def store_packed(ref, full):
    half = full.shape[0] // 2
    mixed, side, diag = pack_symmetric(full)
    ref[0:half, :] = mixed
    ref[half : 2 * half, :] = side
    ref[2 * half : 2 * half + 8, :] = diag


def dot_t(a, b):
    return lax.dot_general(a, b, (((0,), (0,)), ((), ())), preferred_element_type=f32)


def dot_full(a, b):
    return lax.dot_general(
        a, b, (((1,), (0,)), ((), ())), precision=HIGHEST, preferred_element_type=f32
    )


def bucket_side(table, head):
    side = jnp.int32(0)
    for i in range(head):
        side = jnp.where(table[PLACES + i] == table[PLACES + head], 1, side)
    return side


def gram_kernel(place, momentum, gradient, new_momentum, update, *rest, parts):
    outs = rest[:parts]
    held, slopes, split, total, arrive, leave = rest[parts:]
    layers, height, width = update.shape
    slots = width // HD
    tall = split.shape[1]
    wide = 2 * HD
    blocks = [slice(low, low + tall) for low in range(0, height, tall)]
    loads = []
    for i, rows in enumerate(blocks):
        loads.append(
            (
                pltpu.make_async_copy(momentum.at[:, rows, :], held.at[:, rows, :], arrive.at[0, i]),
                pltpu.make_async_copy(gradient.at[:, rows, :], slopes.at[:, rows, :], arrive.at[1, i]),
            )
        )
        for load in loads[-1]:
            load.start()
    stores = []
    for i, rows in enumerate(blocks):
        for load in loads[i]:
            load.wait()
        for head in range(layers * slots):
            layer = head // slots
            cols = slice((head % slots) * HD, (head % slots + 1) * HD)
            slope = slopes[layer, rows, cols]
            fresh = beta_momentum * held[layer, rows, cols] + slope
            held[layer, rows, cols] = fresh
            change = slope + beta_momentum * fresh
            update[layer, rows, cols] = change
            side = bucket_side(place, head)
            for k, plane in enumerate(split_three(change)):
                start = pl.multiple_of(k * wide + side * HD, HD)
                split[place[PLACES + head], :, pl.ds(start, HD)] = plane
        stores.append(
            pltpu.make_async_copy(held.at[:, rows, :], new_momentum.at[:, rows, :], leave.at[i])
        )
        stores[-1].start()
        for bucket in range(parts):
            planes = split[bucket]
            two = planes[:, wide : 2 * wide]
            mixed = dot_t(planes[:, :wide], planes)
            rough = mixed[:, :wide] + dot_t(two, two)
            rough = rough + 2.0 * (mixed[:, wide : 2 * wide] + mixed[:, 2 * wide :])
            if i > 0:
                rough = total[bucket] + rough
            if i + 1 < len(blocks):
                total[bucket] = rough
                continue
            mixed, side, diag = pack_symmetric(0.5 * (rough + rough.T))
            away = bucket ^ place[0]
            for k in range(parts):

                @pl.when(away == k)
                def _():
                    outs[k][0:HD, :] = mixed
                    outs[k][HD : 2 * HD, :] = side
                    outs[k][2 * HD : 2 * HD + 8, :] = diag

    for store in stores:
        store.wait()


def local_grams(place, momentum, gradient, parts):
    shape = momentum.shape
    tall = min(shape[1], ROWS)
    blocks = shape[1] // tall
    packed = (2 * HD + 8, HD)
    anywhere = pl.BlockSpec(memory_space=pl.ANY)
    return pl.pallas_call(
        functools.partial(gram_kernel, parts=parts),
        in_specs=[SM, anywhere, anywhere],
        out_specs=[anywhere] + [VM] * (parts + 1),
        scratch_shapes=[
            pltpu.VMEM(shape, f32),
            pltpu.VMEM(shape, f32),
            pltpu.VMEM((parts, tall, 6 * HD), bf16),
            pltpu.VMEM((parts, 2 * HD, 2 * HD), f32),
            pltpu.SemaphoreType.DMA((2, blocks)),
            pltpu.SemaphoreType.DMA((blocks,)),
        ],
        out_shape=[jax.ShapeDtypeStruct(shape, f32), pltpu.VMEM(shape, f32)]
        + [pltpu.VMEM(packed, f32)] * parts,
        compiler_params=pltpu.CompilerParams(vmem_limit_bytes=16 * MIB),
        name="grams",
    )(place, hbm(momentum), hbm(gradient))


def series_kernel(*refs, step_scale):
    *pieces, sums, out = refs
    packed = pieces[0][...]
    for ref in pieces[1:]:
        packed = packed + ref[...]
    total = unpack_symmetric(packed)
    rows, cols = grid_masks(total.shape[0])
    on_diag = rows == cols
    trace = jnp.sum(jnp.where(on_diag, total, 0.0), keepdims=True)
    scale = 1.0 / (jnp.sqrt(trace) + frob_epsilon)
    gram = total * (scale * scale)
    product = None
    for iteration in range(NS_ITERS):
        square = dot_full(gram, gram)
        factor = cube_coeff * gram + fifth_coeff * square
        factor = factor + jnp.where(on_diag, first_coeff, 0.0)
        product = factor if product is None else dot_full(product, factor)
        if iteration + 1 < NS_ITERS:
            gram = dot_full(dot_full(gram, factor), factor)
    store_packed(out, product * (scale * step_scale))
    first = pieces[0].shape[0] - 7
    out[first : first + sums.shape[0], :] = sums[...]


def hbm(value):
    return pltpu.with_memory_space_constraint(value, pltpu.HBM)


def vmem(value):
    return pltpu.with_memory_space_constraint(value, pltpu.VMEM)


def series(pieces, sums, step_scale):
    high, wide = pieces[0].shape
    return pl.pallas_call(
        functools.partial(series_kernel, step_scale=step_scale),
        in_specs=[VM] * (len(pieces) + 1),
        out_specs=VM,
        out_shape=pltpu.VMEM((high, wide), f32),
        compiler_params=pltpu.CompilerParams(vmem_limit_bytes=5 * MIB),
        name="series",
    )(*[vmem(p) for p in pieces], vmem(sums))


def split_three(value):
    one = value.astype(bf16)
    left = value - one.astype(f32)
    two = left.astype(bf16)
    return one, two, (left - two.astype(f32)).astype(bf16)


def head_pair(update, rows, spots):
    pair = [update[layer, rows, cols] for layer, cols in spots]
    one, two, three = split_three(jnp.concatenate(pair, axis=1))
    return jnp.concatenate([one, one, one, two, two, three], axis=1)


def head_spots(table, bucket, slots, count):
    spots = []
    for side in range(2):
        head = head_of(table, 2 * bucket + side, count)
        spots.append((head // slots, pl.ds(pl.multiple_of(head % slots * HD, HD), HD)))
    return spots


def lead_kernel(place, *refs, parts, slots, heads):
    packed = refs[:parts]
    update, master, weights, factors = refs[parts:]
    wide = 2 * HD
    for k in range(parts):
        planes = split_three(unpack_symmetric(packed[k][0 : 2 * HD + 8, :]))
        away = k ^ place[0]
        for spot, plane in enumerate((0, 1, 2, 0, 1, 0)):
            factors[away, spot * wide : (spot + 1) * wide, :] = planes[plane]

    store_weights(place, factors, update, master, weights, slots, range(heads))


def store_weights(place, factors, update, master, weights, slots, heads):
    layers, height, _ = master.shape
    tall = min(height, ROWS)
    for spot, head in enumerate(heads):
        bucket = place[PLACES + head]
        start = pl.multiple_of(bucket_side(place, head) * HD, HD)
        factor = factors[bucket, :, pl.ds(start, HD)]
        spots = head_spots(place, bucket, slots, layers * slots)
        cols = slice(head * HD, (head + 1) * HD)
        for low in range(0, height, tall):
            rows = slice(low, low + tall)
            value = head_pair(update, rows, spots)
            ortho = jnp.dot(value, factor, preferred_element_type=f32)
            rounded = (master[0, rows, cols] - ortho).astype(bf16)
            weights[rows, spot * HD : (spot + 1) * HD] = rounded


def lead_weights(place, packed, update, master, chunks):
    _, height, width = master.shape
    parts = len(packed)
    slots = width // HD
    return pl.pallas_call(
        functools.partial(lead_kernel, parts=parts, slots=slots, heads=slots // chunks),
        in_specs=[SM] + [VM] * (parts + 2),
        out_specs=[VM, VM],
        out_shape=[
            pltpu.VMEM((height, width // chunks), bf16),
            pltpu.VMEM((parts, 12 * HD, 2 * HD), bf16),
        ],
        compiler_params=pltpu.CompilerParams(vmem_limit_bytes=9 * MIB),
        name="lead",
    )(place, *[vmem(p) for p in packed], vmem(update), vmem(master))


def next_kernel(place, factors, update, master, weights, *, slots, heads):
    store_weights(place, factors, update, master, weights, slots, heads)


def next_weights(place, factors, update, master, chunks, chunk):
    _, height, width = master.shape
    slots = width // HD
    share = slots // chunks
    heads = range(chunk * share, (chunk + 1) * share)
    return pl.pallas_call(
        functools.partial(next_kernel, slots=slots, heads=heads),
        in_specs=[SM] + [VM] * 3,
        out_specs=VM,
        out_shape=pltpu.VMEM((height, width // chunks), bf16),
        compiler_params=pltpu.CompilerParams(vmem_limit_bytes=9 * MIB),
        name="next",
    )(place, vmem(factors), vmem(update), vmem(master))


def apply_kernel(place, factors, update, master, new_master, changes, fresh, arrive, leave):
    layers, height, width = master.shape
    slots = width // HD
    tall = min(height, ROWS)
    parts = factors.shape[0]
    blocks = [slice(low, low + tall) for low in range(0, height, tall)]
    loads = []
    for i, rows in enumerate(blocks):
        loads.append(
            (
                pltpu.make_async_copy(update.at[:, rows, :], changes.at[:, rows, :], arrive.at[0, i]),
                pltpu.make_async_copy(master.at[:, rows, :], fresh.at[:, rows, :], arrive.at[1, i]),
            )
        )
        for load in loads[-1]:
            load.start()
    spots = [head_spots(place, bucket, slots, layers * slots) for bucket in range(parts)]
    stores = []
    for i, rows in enumerate(blocks):
        for load in loads[i]:
            load.wait()
        for bucket in range(parts):
            value = head_pair(changes, rows, spots[bucket])
            ortho = jnp.dot(value, factors[bucket], preferred_element_type=f32)
            for side, (layer, cols) in enumerate(spots[bucket]):
                part = ortho[:, side * HD : (side + 1) * HD]
                fresh[layer, rows, cols] = fresh[layer, rows, cols] - part
        stores.append(
            pltpu.make_async_copy(fresh.at[:, rows, :], new_master.at[:, rows, :], leave.at[i])
        )
        stores[-1].start()
    for store in stores:
        store.wait()


def apply_update(place, factors, update, master):
    blocks = master.shape[1] // min(master.shape[1], ROWS)
    anywhere = pl.BlockSpec(memory_space=pl.ANY)
    return pl.pallas_call(
        apply_kernel,
        in_specs=[SM, VM, anywhere, anywhere],
        out_specs=anywhere,
        scratch_shapes=[
            pltpu.VMEM(master.shape, f32),
            pltpu.VMEM(master.shape, f32),
            pltpu.SemaphoreType.DMA((2, blocks)),
            pltpu.SemaphoreType.DMA((blocks,)),
        ],
        out_shape=jax.ShapeDtypeStruct(master.shape, f32),
        compiler_params=pltpu.CompilerParams(vmem_limit_bytes=13 * MIB),
        name="apply",
    )(place, vmem(factors), hbm(update), hbm(master))


def norm_kernel(place, *refs, parts, base, features):
    pieces = refs[:parts]
    packed = refs[parts : 2 * parts]
    gain, out, sums = refs[2 * parts :]
    height, width = pieces[0].shape
    high = packed[0].shape[0] - 8
    for k in range(parts):
        sums[k] = lax.rsqrt(packed[k][high : high + 8, :] / features + rms_epsilon)
    for k in range(parts):
        away = k ^ place[0] ^ place[1]
        inverse = sums[away]
        for low in range(0, height, HD):
            spot = 1 + (base + low) // HD
            column = jnp.broadcast_to(inverse[spot : spot + 1, :], (HD, HD)).T
            for left in range(0, width, HD):
                cols = slice(left, left + HD)
                own = pl.ds(pl.multiple_of(place[0] * width + left, HD), HD)
                values = pieces[k][low : low + HD, cols].astype(f32)
                out[away, low : low + HD, cols] = (values * column * gain[:, own]).astype(bf16)


def normalise(place, pieces, packed, gain, base, features):
    parts = len(packed)
    height, width = pieces[0].shape
    return pl.pallas_call(
        functools.partial(norm_kernel, parts=parts, base=base, features=features),
        in_specs=[SM] + [VM] * (2 * parts + 1),
        out_specs=VM,
        out_shape=pltpu.VMEM((parts, height, width), bf16),
        scratch_shapes=[pltpu.VMEM((parts, 8, HD), f32)],
        compiler_params=pltpu.CompilerParams(vmem_limit_bytes=5 * MIB),
        name="normalise",
    )(place, *[vmem(p) for p in pieces], *[vmem(p) for p in packed], vmem(gain))


def project_kernel(place, near, far, *refs, members, parts):
    weights = refs[:members]
    outs = refs[members : members + parts]
    whole = refs[-1]
    height = weights[0].shape[0]
    for k in range(members):
        start = pl.multiple_of((k ^ place[2]) * height, height)
        whole[pl.ds(start, height), :] = weights[k][...]
    for m in range(parts):
        both = jnp.concatenate([near[m], far[m]], axis=0)
        part = jnp.dot(both, whole[...], preferred_element_type=f32)
        if m == 0:
            outs[m][...] = part
        else:
            encode(outs[m], part)


def encode(out, value):
    height = value.shape[0]
    top = jnp.max(jnp.abs(value), axis=0, keepdims=True)
    power = jnp.ceil(jnp.log2(jnp.maximum(top, LEAST)) - CODE_BITS)
    code = jnp.round(value * jnp.exp2(-power))
    out[0:height, :] = code.astype(jnp.int32).astype(jnp.int16)
    tail = jnp.broadcast_to(power, (CODE_ROWS, value.shape[1]))
    out[height : height + CODE_ROWS, :] = tail.astype(jnp.int32).astype(jnp.int16)


def finish_kernel(*refs, chunks, parts):
    out = refs[-1]
    for c in range(chunks):
        own, *codes = refs[c * parts : (c + 1) * parts]
        height, width = own.shape
        total = own[...]
        for code in codes:
            power = code[height : height + CODE_ROWS, :].astype(jnp.int32).astype(f32)
            value = code[0:height, :].astype(jnp.int32).astype(f32)
            total = total + value * jnp.exp2(power[0:1, :])
        out[:, c * width : (c + 1) * width] = total.astype(bf16)


def finish(pieces):
    chunks = len(pieces)
    parts = len(pieces[0])
    height, width = pieces[0][0].shape
    return pl.pallas_call(
        functools.partial(finish_kernel, chunks=chunks, parts=parts),
        in_specs=[VM] * (chunks * parts),
        out_shape=jax.ShapeDtypeStruct((height, chunks * width), bf16),
        compiler_params=pltpu.CompilerParams(vmem_limit_bytes=5 * MIB),
        name="finish",
    )(*[vmem(p) for piece in pieces for p in piece])


def project(place, near, far, weights):
    parts, height, width = near.shape
    height *= 2
    cols = weights[0].shape[1]
    code = pltpu.VMEM((height + CODE_ROWS, cols), jnp.int16)
    return pl.pallas_call(
        functools.partial(project_kernel, members=len(weights), parts=parts),
        in_specs=[SM] + [VM] * (2 + len(weights)),
        out_specs=[VM] * parts,
        out_shape=[pltpu.VMEM((height, cols), f32)] + [code] * (parts - 1),
        scratch_shapes=[pltpu.VMEM((width, cols), bf16)],
        compiler_params=pltpu.CompilerParams(vmem_limit_bytes=5 * MIB),
        name="project",
    )(place, vmem(near), vmem(far), *[vmem(w) for w in weights])


def after(value, other):
    return lax.optimization_barrier((value, other))[0]


def per_device(master, momentum, gradient, bucket_table, tokens, norm_gain, *, dp, tp):
    _, height, _ = master.shape
    share = tokens.shape[1]
    features = norm_gain.shape[0]
    count = bucket_table.shape[1]
    parts = tp
    members = dp // parts
    assert count // 2 == parts and share * tp == features and height * dp == features
    mine = lax.axis_index("dp")
    column = lax.axis_index("tensor")
    row = mine // members
    spot = jnp.stack([row, column, mine % members]).astype(jnp.int32)
    place = jnp.concatenate([spot, bucket_table[0]])

    def swap_dp(value, bits):
        return lax.ppermute(value, "dp", [(i, i ^ bits) for i in range(dp)])

    def swap_tensor(value, bits):
        return lax.ppermute(value, "tensor", [(i, i ^ bits) for i in range(tp)])

    half = tokens.shape[0] // 2
    flips = (0, tp // 2)
    far = swap_tensor(lax.slice_in_dim(tokens, half, 2 * half, axis=0), tp // 2)

    def turn(value, flip):
        pairs = []
        for q in range(parts):
            for r in range(members):
                for j in range(tp):
                    target = ((j ^ flip) * members + r) * tp + (q ^ flip)
                    pairs.append(((q * members + r) * tp + j, target))
        return lax.ppermute(value, ("dp", "tensor"), pairs)

    new_momentum, update, *grams = local_grams(place, momentum, gradient, parts)

    local_f = tokens.astype(f32)
    sums = jnp.sum(local_f * local_f, axis=1)
    bits = tp // 2
    while bits:
        sums = sums + swap_tensor(sums, bits)
        bits //= 2

    near = lax.slice_in_dim(after(tokens, grams[0]), 0, half, axis=0)
    sent = [turn(near, flips[0]), turn(after(far, grams[0]), flips[1])]
    total = grams[0]
    for k in range(1, parts):
        total = total + swap_dp(grams[k], k * members)
    pieces = [total]
    bits = 1
    while bits < members:
        pieces = [sum(pieces), swap_dp(sum(pieces), bits)]
        bits *= 2
    step_scale = learn_rate * math.sqrt(max(1.0, features / (2.0 * HD)))
    own = series(pieces, sums.reshape(-1, HD), step_scale)

    packed = [own] + [swap_dp(own, k * members) for k in range(1, parts)]
    lead, factors = lead_weights(place, packed, update, master, CHUNKS)
    gain = norm_gain[None, :]

    def shared(side, start):
        held = {side * (tp // 2): after(sent[side], own)}
        bits = tp // 2
        while bits:
            fresh = {}
            for offset, value in held.items():
                if bits < tp // 2:
                    value = after(value, last if offset == side * (tp // 2) else start)
                fresh[offset ^ bits] = swap_tensor(value, bits)
            held.update(fresh)
            bits //= 2
        halves = [held[offset] for offset in range(parts)]
        return normalise(place, halves, packed, gain, side * half, features)

    others = [next_weights(place, factors, update, master, CHUNKS, c) for c in range(1, CHUNKS)]
    last = (others or [lead])[-1]
    near_normed = shared(0, last)
    normed = (near_normed, shared(1, near_normed))

    pieces = []
    for piece in [lead] + others:
        gathered = [piece] + [swap_dp(piece, k) for k in range(1, members)]
        partial = project(place, *normed, gathered)
        sums_of = [swap_dp(partial[k], k * members) for k in range(1, parts)]
        pieces.append([partial[0]] + sums_of)
    new_master = apply_update(place, factors, update, master)
    return (new_master, new_momentum, finish(pieces))


def solution(mesh):
    placed = (
        P(None, "dp", "tensor"),
        P(None, "dp", "tensor"),
        P(None, "dp", "tensor"),
        P("tensor", None),
        P("dp", "tensor"),
        P(),
    )

    def step(*args):
        return per_device(*args, dp=mesh.shape["dp"], tp=mesh.shape["tensor"])

    return jax.shard_map(
        step,
        mesh=mesh,
        in_specs=placed,
        out_specs=(P(None, "dp", "tensor"), P(None, "dp", "tensor"), P("dp", "tensor")),
        check_vma=False,
    )
```
